256 devices in a mesh: lon: 64 (over x, y_hi, z), lat: 4 (over y_lo, core).
Axes of the slice: x: 4, y: 4 (y_hi: 2, y_lo: 2; y = y_hi * 2 + y_lo), z: 8, core: 2. Of those that a mesh axis runs over, the one named last changes fastest.
Arguments:
- first_block_input: bfloat16 [128, 2048, 192], P('lat', 'lon'), may hold values from -6 to 6
- first_block_preactivation: bfloat16 [128, 2048, 192], P('lat', 'lon'), may hold values from -8 to 8
- second_block_input: bfloat16 [128, 2048, 192], P('lat', 'lon'), may hold values from -6 to 6
- second_block_preactivation: bfloat16 [128, 2048, 192], P('lat', 'lon'), may hold values from -8 to 8
- output_gradient_final: bfloat16 [128, 2048, 192], P('lat', 'lon'), may hold values from -6 to 6
- first_block_conv_one: bfloat16 [9, 192, 192], replicated, may hold values from -0.15625 to 0.15625
- first_block_conv_two: bfloat16 [9, 192, 192], replicated, may hold values from -0.15625 to 0.15625
- second_block_conv_one: bfloat16 [9, 192, 192], replicated, may hold values from -0.15625 to 0.15625
- second_block_conv_two: bfloat16 [9, 192, 192], replicated, may hold values from -0.15625 to 0.15625
Outputs:
- first_block_input_gradient: bfloat16 [128, 2048, 192], P('lat', 'lon')
- first_block_conv_one_gradient: float32 [9, 192, 192], replicated
- first_block_conv_two_gradient: float32 [9, 192, 192], replicated
- second_block_conv_one_gradient: float32 [9, 192, 192], replicated
- second_block_conv_two_gradient: float32 [9, 192, 192], replicated
The draws below stay inside these ranges and needn't reach their ends.
All inputs are finite; a program needn't handle non-finite values.
Results may differ from the reference program's by a relative error of at most 0.0061.
Values may be sent and summed in bfloat16 or wider, within the bound.
A program may use at most 128 MiB of HBM per device.

```python
import jax
import jax.numpy as jnp
from jax import lax

C = 192
DILATION_FIRST = 16
DILATION_SECOND = 32
NLAT = 128
NLON = 2048


def block_levels(rng, dims, split, least, high):
    gain = 1.0
    for axis_at, blocks in split:
        heights = jax.random.uniform(jax.random.fold_in(jax.random.fold_in(rng, 6), axis_at), (blocks,), jnp.float32, least / len(split), high / len(split))
        gain = gain * jnp.repeat(jnp.exp(heights), dims[axis_at] // blocks).reshape((-1,) + (1,) * (len(dims) - 1 - axis_at))
    return gain


def gaussian(stream_key, extent, spread, limit, cuts=(), kind=jnp.bfloat16):
    loudness = block_levels(stream_key, extent, cuts, -0.22, 0.18) if cuts else 1.0
    entries = jax.random.normal(stream_key, extent, jnp.float32) * spread * loudness
    return jnp.minimum(jnp.maximum(entries, -limit), limit).astype(kind)


def setup_inputs(seed: int = 0) -> dict:
    seeds = jax.random.split(jax.random.key(seed), 10)
    first_block_input = gaussian(seeds[0], (NLAT, NLON, C), 1.0, 6.0, ((0, 4), (1, 64)))
    first_block_preactivation = gaussian(seeds[1], (NLAT, NLON, C), 1.5, 8.0, ((0, 4), (1, 64)))
    second_block_input = gaussian(seeds[2], (NLAT, NLON, C), 1.0, 6.0, ((0, 4), (1, 64)))
    second_block_preactivation = gaussian(seeds[3], (NLAT, NLON, C), 1.5, 8.0, ((0, 4), (1, 64)))
    output_gradient_final = gaussian(seeds[4], (NLAT, NLON, C), 1.0, 6.0, ((0, 4), (1, 64)))
    first_block_conv_one = gaussian(seeds[5], (9, C, C), (9 * C) ** -0.5, 0.15625)
    first_block_conv_two = gaussian(seeds[6], (9, C, C), (9 * C) ** -0.5, 0.15625)
    second_block_conv_one = gaussian(seeds[7], (9, C, C), (9 * C) ** -0.5, 0.15625)
    second_block_conv_two = gaussian(seeds[8], (9, C, C), (9 * C) ** -0.5, 0.15625)
    return dict(first_block_input=first_block_input, first_block_preactivation=first_block_preactivation, second_block_input=second_block_input, second_block_preactivation=second_block_preactivation, output_gradient_final=output_gradient_final, first_block_conv_one=first_block_conv_one, first_block_conv_two=first_block_conv_two, second_block_conv_one=second_block_conv_one, second_block_conv_two=second_block_conv_two)


tap_offsets = [(row_tap, col_tap) for row_tap in (-1, 0, 1) for col_tap in (-1, 0, 1)]

def shifted(values, row_shift, col_shift):
    values = jnp.roll(values, -col_shift, axis=1)
    if row_shift > 0:
        filler = jnp.zeros((row_shift,) + values.shape[1:], values.dtype)
        return jnp.concatenate([values[row_shift:], filler], 0)
    if row_shift < 0:
        filler = jnp.zeros((-row_shift,) + values.shape[1:], values.dtype)
        return jnp.concatenate([filler, values[:row_shift]], 0)
    return values

def weight_grad(source, gradient, dilation):
    return jnp.stack([lax.dot_general(shifted(source, row_tap * dilation, col_tap * dilation), gradient, (((0, 1), (0, 1)), ((), ())), preferred_element_type=jnp.float32) for row_tap, col_tap in tap_offsets])

def transpose_conv(gradient, weights, dilation):
    total = jnp.zeros(gradient.shape, jnp.float32)
    for position, (row_tap, col_tap) in enumerate(tap_offsets):
        moved = shifted(gradient, -row_tap * dilation, -col_tap * dilation)
        total = total + lax.dot_general(moved, weights[position], (((2,), (1,)), ((), ())), preferred_element_type=jnp.float32)
    return total

def residual_block_backward(entry, hidden_pre, gradient, first, second, dilation):
    pre = hidden_pre.astype(jnp.float32)
    sigma = jax.nn.sigmoid(pre)
    hidden = (pre * sigma).astype(jnp.bfloat16)
    grad_second = weight_grad(hidden, gradient, dilation)
    grad_hidden = transpose_conv(gradient, second, dilation)
    grad_pre = (grad_hidden * sigma * (1.0 + pre * (1.0 - sigma))).astype(jnp.bfloat16)
    grad_first = weight_grad(entry, grad_pre, dilation)
    first_block_input_gradient = (gradient.astype(jnp.float32) + transpose_conv(grad_pre, first, dilation)).astype(jnp.bfloat16)
    return (first_block_input_gradient, grad_first, grad_second)

def reference(first_block_input, first_block_preactivation, second_block_input, second_block_preactivation, output_gradient_final, first_block_conv_one, first_block_conv_two, second_block_conv_one, second_block_conv_two):
    between_blocks_gradient, second_block_conv_one_gradient, second_block_conv_two_gradient = residual_block_backward(second_block_input, second_block_preactivation, output_gradient_final, second_block_conv_one, second_block_conv_two, DILATION_SECOND)
    first_block_input_gradient, first_block_conv_one_gradient, first_block_conv_two_gradient = residual_block_backward(first_block_input, first_block_preactivation, between_blocks_gradient, first_block_conv_one, first_block_conv_two, DILATION_FIRST)
    return (first_block_input_gradient, first_block_conv_one_gradient, first_block_conv_two_gradient, second_block_conv_one_gradient, second_block_conv_two_gradient)
```

```python
import jax
import jax.numpy as jnp
from jax import lax
from jax.experimental import pallas as pl
from jax.experimental.pallas import tpu as pltpu
from jax.sharding import PartitionSpec as P

C = 192
DILATION_FIRST = 16
DILATION_SECOND = 32
MESH = pl.DeviceIdType.MESH
BF = jnp.bfloat16
F32 = jnp.float32
T = 32
ROWS = 3072
HALF, QUART, SHARD = ROWS // 2, ROWS // 8, ROWS // 32


class Place:
    def __init__(self):
        lon, lat = lax.axis_index("lon"), lax.axis_index("lat")
        self.lon, self.lat = lon, lat
        self.x, self.yh, self.z = lon // 16, (lon // 8) % 2, lon % 8
        self.yl, self.core = lat // 2, lat % 2
        self.y = self.yh * 2 + self.yl
        self.east = {"lon": (lon + 1) % 64, "lat": lat}
        self.west = {"lon": (lon + 63) % 64, "lat": lat}
        self.north = {"lon": lon, "lat": jnp.minimum(lat + 1, 3)}
        self.south = {"lon": lon, "lat": jnp.maximum(lat - 1, 0)}
        self.twin = {"lon": lon, "lat": lat + 1 - 2 * self.core}
        self.has_north, self.has_south = lat < 3, lat > 0

    def at_x(self, k):
        x = (self.x + k) % 4
        return x, {"lon": x * 16 + self.lon % 16, "lat": self.lat}

    def at_y(self, k):
        y = (self.y + k) % 4
        lon = self.x * 16 + (y // 2) * 8 + self.z
        return y, {"lon": lon, "lat": (y % 2) * 2 + self.core}

    def at_z(self, k):
        z = (self.z + k) % 8
        return z, {"lon": self.lon - self.z + z, "lat": self.lat}


def remote(src, dst, send, recv, where):
    return pltpu.make_async_remote_copy(
        src_ref=src, dst_ref=dst, send_sem=send, recv_sem=recv, device_id=where, device_id_type=MESH
    )


class Sems:
    def __init__(self, send, recv):
        self.send, self.recv, self.n = send, recv, 0

    def take(self):
        k = self.n
        self.n += 1
        return self.send.at[k], self.recv.at[k]


class Reduction:
    def __init__(self, place, sems, local, from_twin, xs, xr, ys, yr, zs, zr, out):
        self.p, self.local, self.from_twin = place, local, from_twin
        self.xs, self.xr, self.ys, self.yr, self.zs, self.zr, self.out = xs, xr, ys, yr, zs, zr, out
        p = place
        other = pl.multiple_of((1 - p.core) * HALF, HALF)
        mine = pl.multiple_of(p.core * HALF, HALF)
        xo = pl.multiple_of(mine + p.x * QUART, QUART)
        yo = pl.multiple_of(xo + p.y * SHARD, SHARD)
        self.mine, self.xo, self.yo = mine, xo, yo
        self.twin = [remote(local.at[pl.ds(other, HALF)], from_twin, *sems.take(), p.twin)]
        self.to_x = []
        for k in (1, 2, 3):
            x, where = p.at_x(k)
            src = xs.at[pl.ds(pl.multiple_of(x * QUART, QUART), QUART)]
            self.to_x.append(remote(src, xr.at[k - 1], *sems.take(), where))
        self.to_y = []
        for k in (1, 2, 3):
            y, where = p.at_y(k)
            src = ys.at[pl.ds(pl.multiple_of(y * SHARD, SHARD), SHARD)]
            self.to_y.append(remote(src, yr.at[k - 1], *sems.take(), where))
        self.to_z = [remote(zs, zr.at[p.z], *sems.take(), p.at_z(k)[1]) for k in range(1, 8)]
        ref = out.at[pl.ds(yo, SHARD)]
        self.all_y = [remote(ref, ref, *sems.take(), p.at_y(k)[1]) for k in (1, 2, 3)]
        ref = out.at[pl.ds(xo, QUART)]
        self.all_x = [remote(ref, ref, *sems.take(), p.at_x(k)[1]) for k in (1, 2, 3)]
        ref = out.at[pl.ds(mine, HALF)]
        self.all_twin = [remote(ref, ref, *sems.take(), p.twin)]
        self.step = 0

    def go(self):
        getattr(self, f"step{self.step}")()
        self.step += 1

    def start(self, copies):
        for copy in copies:
            copy.start()

    def arrive(self, copies):
        for copy in copies:
            copy.wait_recv()

    def step0(self):
        self.start(self.twin)

    def step1(self):
        self.arrive(self.twin)

        @pl.loop(0, HALF // 128)
        def _(i):
            rows = pl.ds(pl.multiple_of(i * 128, 128), 128)
            own = self.local[pl.ds(pl.multiple_of(self.mine + i * 128, 128), 128)]
            self.xs[rows] = (own + self.from_twin[rows]).astype(BF)

        self.start(self.to_x)

    def step2(self):
        self.arrive(self.to_x)
        base = pl.multiple_of(self.p.x * QUART, QUART)
        total = self.xs[pl.ds(base, QUART)].astype(F32)
        for k in range(3):
            total = total + self.xr[k].astype(F32)
        self.ys[...] = total
        self.start(self.to_y)

    def step3(self):
        self.arrive(self.to_y)
        total = self.ys[pl.ds(pl.multiple_of(self.p.y * SHARD, SHARD), SHARD)]
        for k in range(3):
            total = total + self.yr[k]
        total = total.astype(BF)
        self.zs[...] = total
        self.zr[self.p.z] = total
        self.start(self.to_z)

    def step4(self):
        self.arrive(self.to_z)
        total = self.zr[0].astype(F32)
        for k in range(1, 8):
            total = total + self.zr[k].astype(F32)
        self.out[pl.ds(self.yo, SHARD)] = total.astype(BF)
        self.start(self.all_y)

    def step5(self):
        self.arrive(self.all_y)
        self.start(self.all_x)

    def step6(self):
        self.arrive(self.all_x)
        self.start(self.all_twin)

    def step7(self):
        self.arrive(self.all_twin)

    def drain(self):
        for copies in (self.twin, self.to_x, self.to_y, self.to_z, self.all_y, self.all_x, self.all_twin):
            for copy in copies:
                copy.wait_send()


def pack_rows(v, half):
    return jnp.concatenate([v[:half, :, 128:], v[half:, :, 128:]], axis=-1)


class LonHalo:
    def __init__(self, place, sems, tile, packed, plus, minus, got_plus, got_minus, d):
        self.tile, self.packed, self.plus, self.minus, self.d = tile, packed, plus, minus, d
        self.got_plus, self.got_minus = got_plus, got_minus
        low, high = pl.ds(0, d), pl.ds(T - d, d)
        wide = pl.ds(0, 128)
        self.copies = [
            remote(tile.at[:, high, wide], plus.at[:, low, wide], *sems.take(), place.east),
            remote(tile.at[:, low, wide], minus.at[:, high, wide], *sems.take(), place.west),
            remote(packed.at[:, high], got_plus, *sems.take(), place.east),
            remote(packed.at[:, low], got_minus, *sems.take(), place.west),
        ]

    def start(self):
        for copy in self.copies[:2]:
            copy.start()
        self.packed[...] = pack_rows(self.tile[...], T // 2)
        for copy in self.copies[2:]:
            copy.start()
        d = self.d
        if d < T:
            self.plus[:, d:, :] = self.tile[:, : T - d, :]
            self.minus[:, : T - d, :] = self.tile[:, d:, :]

    def arrive(self):
        for copy in self.copies:
            copy.wait_recv()
        d, h = self.d, T // 2
        self.plus[:h, :d, 128:] = self.got_plus[:, :, :64]
        self.plus[h:, :d, 128:] = self.got_plus[:, :, 64:]
        self.minus[:h, T - d :, 128:] = self.got_minus[:, :, :64]
        self.minus[h:, T - d :, 128:] = self.got_minus[:, :, 64:]

    def drain(self):
        for copy in self.copies:
            copy.wait_send()


def pack_columns(v):
    return jnp.concatenate([v[:, : T // 2, 128:], v[:, T // 2 :, 128:]], axis=-1)


class LatPair:
    def __init__(self, place, copies_north, copies_south):
        self.p, self.to_north, self.to_south = place, copies_north, copies_south

    def start(self):
        @pl.when(self.p.has_north)
        def _():
            for copy in self.to_north:
                copy.start()

        @pl.when(self.p.has_south)
        def _():
            for copy in self.to_south:
                copy.start()

    def arrive(self):
        @pl.when(self.p.has_south)
        def _():
            for copy in self.to_north:
                copy.wait_recv()

        @pl.when(self.p.has_north)
        def _():
            for copy in self.to_south:
                copy.wait_recv()

    def drain(self):
        @pl.when(self.p.has_north)
        def _():
            for copy in self.to_north:
                copy.wait_send()

        @pl.when(self.p.has_south)
        def _():
            for copy in self.to_south:
                copy.wait_send()


class Activation:
    def __init__(self, place, sems, wide, packed, got, turned, d):
        self.p, self.wide, self.packed, self.got, self.turned, self.d = place, wide, packed, got, turned, d
        lanes = pl.ds(0, 128)
        top, bottom = pl.ds(d, d), pl.ds(T, d)
        self.halo = LatPair(
            place,
            [
                remote(wide.at[bottom, :, lanes], wide.at[pl.ds(0, d), :, lanes], *sems.take(), place.north),
                remote(packed.at[pl.ds(T - d, d)], got.at[0], *sems.take(), place.north),
            ],
            [
                remote(wide.at[top, :, lanes], wide.at[pl.ds(T + d, d), :, lanes], *sems.take(), place.south),
                remote(packed.at[pl.ds(0, d)], got.at[1], *sems.take(), place.south),
            ],
        )

    def start(self):
        d = self.d

        @pl.loop(0, 4)
        def _(i):
            v = self.wide[pl.ds(d + i * 8, 8)]
            self.packed[pl.ds(i * 8, 8)] = pack_columns(v)

        self.halo.start()

        @pl.when(jnp.logical_not(self.p.has_south))
        def _():
            self.wide[:d] = jnp.zeros((d, T, C), BF)

        @pl.when(jnp.logical_not(self.p.has_north))
        def _():
            self.wide[T + d :] = jnp.zeros((d, T, C), BF)

    def arrive(self):
        d, h = self.d, T // 2
        self.halo.arrive()

        @pl.when(self.p.has_south)
        def _():
            self.wide[:d, :h, 128:] = self.got[0, :, :, :64]
            self.wide[:d, h:, 128:] = self.got[0, :, :, 64:]

        @pl.when(self.p.has_north)
        def _():
            self.wide[T + d :, :h, 128:] = self.got[1, :, :, :64]
            self.wide[T + d :, h:, 128:] = self.got[1, :, :, 64:]

        @pl.loop(0, (T + 2 * d) // 8)
        def _(i):
            v = self.wide[pl.ds(i * 8, 8)].reshape(8 * T, C)
            self.turned[:, pl.ds(pl.multiple_of(i * 8 * T, 8 * T), 8 * T)] = v.T

    def weight_gradient(self, minus, tile, plus, into):
        cells = T * T

        @pl.loop(0, 3)
        def _(r):
            start = pl.multiple_of(r * self.d * T, 512)
            turned = self.turned[:, pl.ds(start, cells)]
            for c, g in enumerate((minus, tile, plus)):
                d = jnp.dot(turned, g[...].reshape(cells, C), preferred_element_type=F32)
                base = pl.multiple_of((3 * r + c) * 288, 32)
                into[pl.ds(base, C)] = d[:, :128]
                into[pl.ds(base + C, C // 2)] = jnp.concatenate([d[: C // 2, 128:], d[C // 2 :, 128:]], axis=1)

        into[9 * 288 :] = jnp.zeros((ROWS - 9 * 288, 128), F32)


class Pull:
    def __init__(self, place, sems, minus, tile, plus, weights, wide_out, packed_out, wide_in, packed_in, total, d):
        self.p, self.g, self.w, self.d = place, (minus, tile, plus), weights, d
        self.wide_out, self.packed_out, self.wide_in, self.packed_in = wide_out, packed_out, wide_in, packed_in
        self.total = total
        self.halo = LatPair(
            place,
            [
                remote(wide_out.at[0], wide_in.at[0], *sems.take(), place.north),
                remote(packed_out.at[0], packed_in.at[0], *sems.take(), place.north),
            ],
            [
                remote(wide_out.at[1], wide_in.at[1], *sems.take(), place.south),
                remote(packed_out.at[1], packed_in.at[1], *sems.take(), place.south),
            ],
        )

    def partial(self, r, row):
        total = None
        for c in range(3):
            g = self.g[c][pl.ds(row, 8)].reshape(8 * T, C)
            term = lax.dot_general(
                g, self.w[3 * (r + 1) + c], (((1,), (1,)), ((), ())), preferred_element_type=F32
            )
            total = term if total is None else total + term
        return total.reshape(8, T, C)

    def send(self):
        d = self.d

        @pl.loop(0, d // 8)
        def _(i):
            for slot, r, first in ((0, 1, T - d), (1, -1, 0)):
                v = self.partial(r, first + i * 8).astype(BF)
                self.wide_out[slot, pl.ds(i * 8, 8)] = v[:, :, :128]
                self.packed_out[slot, pl.ds(i * 8, 8)] = pack_columns(v)

        self.halo.start()

        @pl.when(jnp.logical_not(self.p.has_south))
        def _():
            self.wide_in[0] = jnp.zeros(self.wide_in.shape[1:], BF)
            self.packed_in[0] = jnp.zeros(self.packed_in.shape[1:], BF)

        @pl.when(jnp.logical_not(self.p.has_north))
        def _():
            self.wide_in[1] = jnp.zeros(self.wide_in.shape[1:], BF)
            self.packed_in[1] = jnp.zeros(self.packed_in.shape[1:], BF)

    def stay(self):
        d = self.d

        @pl.loop(0, T // 8)
        def _(i):
            self.total[pl.ds(i * 8, 8)] = self.partial(0, i * 8)

        if d < T:

            @pl.loop(0, (T - d) // 8)
            def _(i):
                self.total[pl.ds(d + i * 8, 8)] += self.partial(1, i * 8)
                self.total[pl.ds(i * 8, 8)] += self.partial(-1, d + i * 8)

    def finish(self, use):
        d = self.d
        self.halo.arrive()

        def got(slot, row):
            w = self.wide_in[slot, pl.ds(row, 8)].astype(F32)
            q = self.packed_in[slot, pl.ds(row, 8)].astype(F32)
            return jnp.concatenate([w, jnp.concatenate([q[:, :, :64], q[:, :, 64:]], axis=1)], axis=-1)

        if d == T:

            @pl.loop(0, T // 8)
            def _(i):
                use(i * 8, self.total[pl.ds(i * 8, 8)] + got(0, i * 8) + got(1, i * 8))

        else:

            @pl.loop(0, d // 8)
            def _(i):
                use(i * 8, self.total[pl.ds(i * 8, 8)] + got(0, i * 8))
                use(T - d + i * 8, self.total[pl.ds(T - d + i * 8, 8)] + got(1, i * 8))


def scratch():
    v = pltpu.VMEM
    shapes = {}
    for b, d in (("1", DILATION_FIRST), ("2", DILATION_SECOND)):
        shapes["a" + b] = v((T, T, C), BF)
        shapes["slope" + b] = v((T, T, C), F32)
        for n in ("w1", "w2"):
            shapes[n + b] = v((9, C, C), BF)
        for n in ("h", "x"):
            shapes[n + b] = v((T + 2 * d, T, C), BF)
            shapes[n + b + "packed"] = v((T, T // 2, 128), BF)
            shapes[n + b + "got"] = v((2, d, T // 2, 128), BF)
            shapes[n + b + "turned"] = v((C, (T + 2 * d) * T), BF)
        for n in ("g", "q"):
            shapes[n + b] = v((T, T, C), BF)
            shapes[n + b + "packed"] = v((T // 2, T, 128), BF)
            for s in ("plus", "minus"):
                shapes[n + b + s] = v((T, T, C), BF)
                shapes[n + b + "got_" + s] = v((T // 2, d, 128), BF)
            for s in ("wide_out", "wide_in"):
                shapes[n + b + s] = v((2, d, T, 128), BF)
            for s in ("packed_out", "packed_in"):
                shapes[n + b + s] = v((2, d, T // 2, 128), BF)
        for n in ("1", "2"):
            m = "r" + n + b
            shapes[m + "local"] = v((ROWS, 128), F32)
            shapes[m + "from_twin"] = v((HALF, 128), F32)
            shapes[m + "xs"] = v((HALF, 128), BF)
            shapes[m + "xr"] = v((3, QUART, 128), BF)
            shapes[m + "ys"] = v((QUART, 128), F32)
            shapes[m + "yr"] = v((3, SHARD, 128), F32)
            shapes[m + "zs"] = v((SHARD, 128), BF)
            shapes[m + "zr"] = v((8, SHARD, 128), BF)
            shapes[m + "out"] = v((ROWS, 128), BF)
    shapes["total"] = v((T, T, C), F32)
    shapes["dx"] = v((T, T, C), BF)
    shapes["load"] = pltpu.SemaphoreType.DMA((9,))
    shapes["store"] = pltpu.SemaphoreType.DMA((5,))
    shapes["send"] = pltpu.SemaphoreType.DMA((160,))
    shapes["recv"] = pltpu.SemaphoreType.DMA((160,))
    return shapes


NAMES = tuple(scratch())


def body(x1, a1, x2, a2, g2, w11, w21, w12, w22, dx_out, r11_out, r21_out, r12_out, r22_out, *refs):
    s = dict(zip(NAMES, refs))
    p = Place()
    loads = {}
    d1, d2 = DILATION_FIRST, DILATION_SECOND
    for k, (name, src, dst) in enumerate(
        (
            ("g2", g2, s["g2"]),
            ("a2", a2, s["a2"]),
            ("x2", x2, s["x2"].at[pl.ds(d2, T)]),
            ("w22", w22, s["w22"]),
            ("a1", a1, s["a1"]),
            ("x1", x1, s["x1"].at[pl.ds(d1, T)]),
            ("w12", w12, s["w12"]),
            ("w21", w21, s["w21"]),
            ("w11", w11, s["w11"]),
        )
    ):
        loads[name] = pltpu.make_async_copy(src, dst, s["load"].at[k])
        loads[name].start()

    barrier = pltpu.get_barrier_semaphore()
    peers = [p.east, p.west, p.twin]
    peers += [p.at_x(k)[1] for k in (1, 2, 3)] + [p.at_y(k)[1] for k in (1, 2, 3)]
    peers += [p.at_z(k)[1] for k in range(1, 8)]
    for where in peers:
        pl.semaphore_signal(barrier, inc=1, device_id=where, device_id_type=MESH)
    for cond, where in ((p.has_north, p.north), (p.has_south, p.south)):

        @pl.when(cond)
        def _():
            pl.semaphore_signal(barrier, inc=1, device_id=where, device_id_type=MESH)

    expected = len(peers) + p.has_north.astype(jnp.int32) + p.has_south.astype(jnp.int32)

    sems = Sems(s["send"], s["recv"])

    def reduction(m):
        names = ("local", "from_twin", "xs", "xr", "ys", "yr", "zs", "zr", "out")
        return Reduction(p, sems, *(s[m + n] for n in names))

    def lon_halo(m, d):
        names = ("", "packed", "plus", "minus", "got_plus", "got_minus")
        return LonHalo(p, sems, *(s[m + n] for n in names), d)

    def pull(m, w, d):
        names = ("minus", "", "plus")
        outs = ("wide_out", "packed_out", "wide_in", "packed_in")
        return Pull(p, sems, *(s[m + n] for n in names), s[w], *(s[m + n] for n in outs), s["total"], d)

    def activation(m, d):
        return Activation(p, sems, *(s[m + n] for n in ("", "packed", "got", "turned")), d)

    red = {m: reduction(m) for m in ("r22", "r12", "r21", "r11")}
    halos = {m: lon_halo(m, d) for m, d in (("g2", d2), ("q2", d2), ("g1", d1), ("q1", d1))}
    pulls = {
        m: pull(m, w, d) for m, w, d in (("g2", "w22", d2), ("q2", "w12", d2), ("g1", "w21", d1), ("q1", "w11", d1))
    }
    acts = {m: activation(m, d) for m, d in (("h2", d2), ("x2", d2), ("h1", d1), ("x1", d1))}

    def gate(b, d):
        @pl.loop(0, T // 4)
        def _(i):
            rows = pl.ds(i * 4, 4)
            pre = s["a" + b][rows].astype(F32)
            sigma = jax.nn.sigmoid(pre)
            s["h" + b][pl.ds(d + i * 4, 4)] = (pre * sigma).astype(BF)
            s["slope" + b][rows] = sigma * (1.0 + pre * (1.0 - sigma))

    def use_pre(b):
        def use(row, v):
            s["q" + b][pl.ds(row, 8)] = (v * s["slope" + b][pl.ds(row, 8)]).astype(BF)

        return use

    def use_x(b, into):
        def use(row, v):
            into[pl.ds(row, 8)] = (s["g" + b][pl.ds(row, 8)].astype(F32) + v).astype(BF)

        return use

    def weight(act, m, r):
        acts[act].weight_gradient(s[m + "minus"], s[m], s[m + "plus"], s[r + "local"])

    loads["g2"].wait()
    pl.semaphore_wait(barrier, expected)
    halos["g2"].start()
    loads["a2"].wait()
    gate("2", d2)
    acts["h2"].start()
    loads["x2"].wait()
    acts["x2"].start()
    loads["a1"].wait()
    gate("1", d1)
    acts["h1"].start()
    loads["x1"].wait()
    acts["x1"].start()
    acts["h2"].arrive()
    for name in ("w22", "w12", "w21", "w11"):
        loads[name].wait()

    halos["g2"].arrive()
    pulls["g2"].send()
    pulls["g2"].stay()
    weight("h2", "g2", "r22")
    red["r22"].go()
    acts["x2"].arrive()
    pulls["g2"].finish(use_pre("2"))
    halos["q2"].start()
    red["r22"].go()
    acts["h1"].arrive()
    acts["x1"].arrive()
    red["r22"].go()

    halos["q2"].arrive()
    pulls["q2"].send()
    pulls["q2"].stay()
    weight("x2", "q2", "r12")
    red["r12"].go()
    red["r22"].go()
    pulls["q2"].finish(use_x("2", s["g1"]))
    halos["g1"].start()
    red["r12"].go()
    red["r22"].go()

    halos["g1"].arrive()
    pulls["g1"].send()
    pulls["g1"].stay()
    weight("h1", "g1", "r21")
    red["r21"].go()
    red["r12"].go()
    red["r22"].go()
    pulls["g1"].finish(use_pre("1"))
    halos["q1"].start()
    red["r21"].go()
    red["r12"].go()
    red["r22"].go()

    halos["q1"].arrive()
    weight("x1", "q1", "r11")
    red["r11"].go()
    pulls["q1"].send()
    pulls["q1"].stay()
    red["r11"].go()
    red["r21"].go()
    red["r12"].go()
    pulls["q1"].finish(use_x("1", s["dx"]))
    stores = [pltpu.make_async_copy(s["dx"], dx_out, s["store"].at[0])]
    stores[0].start()
    red["r22"].go()
    red["r11"].go()
    red["r21"].go()
    red["r12"].go()
    red["r11"].go()
    red["r21"].go()
    red["r12"].go()
    red["r11"].go()
    red["r21"].go()
    red["r12"].go()
    red["r11"].go()
    red["r21"].go()
    red["r11"].go()
    red["r21"].go()
    red["r11"].go()
    for k, (m, out) in enumerate((("r22", r22_out), ("r12", r12_out), ("r21", r21_out), ("r11", r11_out))):
        stores.append(pltpu.make_async_copy(s[m + "out"], out, s["store"].at[1 + k]))
        stores[-1].start()
    for part in (*halos.values(), *red.values()):
        part.drain()
    for part in (*pulls.values(), *acts.values()):
        part.halo.drain()
    for copy in stores:
        copy.wait()


def unpack(packed):
    taps = packed[: 9 * 288].reshape(9, 288, 128)
    rest = taps[:, C:].reshape(9, C // 2, 2, 64).transpose(0, 2, 1, 3).reshape(9, C, 64)
    return jnp.concatenate([taps[:, :C], rest], axis=-1).astype(F32)


def local(x1, a1, x2, a2, g2, w11, w21, w12, w22):
    shapes = scratch()
    anywhere = pl.BlockSpec(memory_space=pl.ANY)
    packed = jax.ShapeDtypeStruct((ROWS, 128), BF)
    dx, *sums = pl.pallas_call(
        body,
        name="backward",
        out_shape=(jax.ShapeDtypeStruct((T, T, C), BF), packed, packed, packed, packed),
        in_specs=[anywhere] * 9,
        out_specs=[anywhere] * 5,
        scratch_shapes=list(shapes.values()),
        compiler_params=pltpu.CompilerParams(
            collective_id=0, has_side_effects=True, vmem_limit_bytes=60 * 1024 * 1024
        ),
    )(x1, a1, x2, a2, g2, w11, w21, w12, w22)
    return (dx, *(unpack(v) for v in sums))


def solution(mesh):
    tile = P("lat", "lon", None)
    return jax.shard_map(
        local,
        mesh=mesh,
        in_specs=(tile,) * 5 + (P(),) * 4,
        out_specs=(tile, P(), P(), P(), P()),
        check_vma=False,
    )
```

```python
import jax
import jax.numpy as jnp
from jax import lax
from jax.experimental import pallas as pl
from jax.experimental.pallas import tpu as pltpu
from jax.sharding import PartitionSpec as P

C = 192
DILATION_FIRST = 16
DILATION_SECOND = 32
MESH = pl.DeviceIdType.MESH
BF = jnp.bfloat16
F32 = jnp.float32
T = 32
ROWS = 3072
HALF, QUART, SHARD = ROWS // 2, ROWS // 8, ROWS // 64


class Place:
    def __init__(self):
        lon, lat = lax.axis_index("lon"), lax.axis_index("lat")
        self.lon, self.lat = lon, lat
        self.x, self.yh, self.z = lon // 16, (lon // 8) % 2, lon % 8
        self.yl, self.core = lat // 2, lat % 2
        self.y = self.yh * 2 + self.yl
        self.east = {"lon": (lon + 1) % 64, "lat": lat}
        self.west = {"lon": (lon + 63) % 64, "lat": lat}
        self.north = {"lon": lon, "lat": jnp.minimum(lat + 1, 3)}
        self.south = {"lon": lon, "lat": jnp.maximum(lat - 1, 0)}
        self.twin = {"lon": lon, "lat": lat + 1 - 2 * self.core}
        self.has_north, self.has_south = lat < 3, lat > 0
        self.ends = (self.z == 0) | (self.z == 7)
        self.inner = (lat == 1) | (lat == 2)
        top = (self.z == 7).astype(jnp.int32)
        half = 1 - top
        self.here = self.yh == half
        away = 2 * top - 1
        beside = (self.x + 4 + away) % 4
        self.column = jnp.where(self.here, self.x, beside)
        self.senders = (self.x * 16 + half * 8 + self.z, ((self.x + 4 - away) % 4) * 16 + top * 8 + self.z)

    def column_first(self, to_senders, to_column):
        @pl.when(self.ends & self.inner)
        def _():
            for k, lon in enumerate(self.senders):
                for lat in range(4):
                    other = jnp.logical_not(self.here & (self.lat == lat)) if k == 0 else self.ends
                    pl.when(other)(lambda lon=lon, lat=lat: to_senders({"lon": lon, "lat": lat}))

        if to_column is not None:

            @pl.when(self.ends)
            def _():
                for yh in range(2):
                    for lat in (1, 2):
                        other = jnp.logical_not(self.here & (self.yh == yh) & (self.lat == lat))
                        lon = self.column * 16 + yh * 8 + self.z
                        pl.when(other)(lambda lon=lon, lat=lat: to_column({"lon": lon, "lat": lat}))

    def at_x(self, k):
        x = (self.x + k) % 4
        return x, {"lon": x * 16 + self.lon % 16, "lat": self.lat}

    def at_y(self, k):
        y = (self.y + k) % 4
        return y, {"lon": self.x * 16 + (y // 2) * 8 + self.z, "lat": (y % 2) * 2 + self.core}

    def at_z(self, k):
        z = (self.z + k) % 8
        return z, {"lon": self.lon - self.z + z, "lat": self.lat}


def remote(src, dst, send, recv, where):
    return pltpu.make_async_remote_copy(
        src_ref=src, dst_ref=dst, send_sem=send, recv_sem=recv, device_id=where, device_id_type=MESH
    )


class Sems:
    def __init__(self, send, recv):
        self.send, self.recv, self.n = send, recv, 0

    def take(self):
        k = self.n
        self.n += 1
        return self.send.at[k], self.recv.at[k]


class Reduction:
    def __init__(self, place, sems, local, from_twin, xs, xr, zs, zr, yr, out):
        self.p, self.local, self.from_twin = place, local, from_twin
        self.xs, self.xr, self.zs, self.zr, self.yr, self.out = xs, xr, zs, zr, yr, out
        p = place
        self.mine = pl.multiple_of(p.core * HALF, HALF)
        other = pl.multiple_of((1 - p.core) * HALF, HALF)
        quarter = pl.multiple_of(self.mine + p.x * QUART, QUART)
        self.shard = pl.ds(pl.multiple_of(quarter + p.z * SHARD, SHARD), SHARD)
        self.twin = [remote(local.at[pl.ds(other, HALF)], from_twin, *sems.take(), p.twin)]
        self.to_x = []
        for k in range(1, 4):
            x, where = p.at_x(k)
            src = xs.at[pl.ds(pl.multiple_of(x * QUART, QUART), QUART)]
            self.to_x.append(remote(src, xr.at[k - 1], *sems.take(), where))
        self.to_z = []
        for k in range(1, 8):
            z, where = p.at_z(k)
            src = zs.at[pl.ds(pl.multiple_of(z * SHARD, SHARD), SHARD)]
            self.to_z.append(remote(src, zr.at[k - 1], *sems.take(), where))
        self.to_y = [remote(yr.at[p.y], yr.at[p.y], *sems.take(), p.at_y(k)[1]) for k in range(1, 4)]
        ref = out.at[self.shard]
        self.all_z = [remote(ref, ref, *sems.take(), p.at_z(k)[1]) for k in range(1, 8)]
        ref = out.at[pl.ds(quarter, QUART)]
        self.all_x = [remote(ref, ref, *sems.take(), p.at_x(k)[1]) for k in range(1, 4)]
        ref = out.at[pl.ds(self.mine, HALF)]
        self.all_twin = [remote(ref, ref, *sems.take(), p.twin)]
        self.step = 0

    def go(self):
        getattr(self, f"step{self.step}")()
        self.step += 1

    def start(self, copies):
        for copy in copies:
            copy.start()

    def arrive(self, copies):
        for copy in copies:
            copy.wait_recv()

    def step0(self):
        self.start(self.twin)

    def step1(self):
        self.arrive(self.twin)

        @pl.loop(0, HALF // 128)
        def _(i):
            rows = pl.ds(pl.multiple_of(i * 128, 128), 128)
            own = self.local[pl.ds(pl.multiple_of(self.mine + i * 128, 128), 128)]
            self.xs[rows] = (own + self.from_twin[rows]).astype(BF)

        self.start(self.to_x)

    def step2(self):
        self.arrive(self.to_x)
        total = self.xs[pl.ds(pl.multiple_of(self.p.x * QUART, QUART), QUART)].astype(F32)
        for k in range(3):
            total = total + self.xr[k].astype(F32)
        self.zs[...] = total.astype(BF)
        self.start(self.to_z)

    def step3(self):
        self.arrive(self.to_z)
        total = self.zs[pl.ds(pl.multiple_of(self.p.z * SHARD, SHARD), SHARD)].astype(F32)
        for k in range(7):
            total = total + self.zr[k].astype(F32)
        self.yr[self.p.y] = total
        self.start(self.to_y)

    def step4(self):
        self.arrive(self.to_y)
        self.out[self.shard] = ((self.yr[0] + self.yr[1]) + (self.yr[2] + self.yr[3])).astype(BF)
        self.start(self.all_z)

    def step5(self):
        self.arrive(self.all_z)
        self.start(self.all_x)

    def step6(self):
        self.arrive(self.all_x)
        self.start(self.all_twin)

    def step7(self):
        self.arrive(self.all_twin)

    def drain(self):
        for copies in (self.twin, self.to_x, self.to_z, self.to_y, self.all_z, self.all_x, self.all_twin):
            for copy in copies:
                copy.wait_send()


def pack_rows(v, half):
    return jnp.concatenate([v[:half, :, 128:], v[half:, :, 128:]], axis=-1)


class LonHalo:
    def __init__(self, place, sems, tile, packed, plus, minus, got_plus, got_minus, d):
        self.p = place
        self.tile, self.packed, self.plus, self.minus, self.d = tile, packed, plus, minus, d
        self.got_plus, self.got_minus = got_plus, got_minus
        low, high = pl.ds(0, d), pl.ds(T - d, d)
        wide = pl.ds(0, 128)
        self.copies = [
            remote(tile.at[:, high, wide], plus.at[:, low, wide], *sems.take(), place.east),
            remote(tile.at[:, low, wide], minus.at[:, high, wide], *sems.take(), place.west),
            remote(packed.at[:, high], got_plus, *sems.take(), place.east),
            remote(packed.at[:, low], got_minus, *sems.take(), place.west),
        ]

    def start(self, turn=None):
        p = self.p
        late = [(p.z == z) if turn is not None else None for z in (7, 0, 7, 0)]

        def go(k):
            if late[k] is None:
                self.copies[k].start()
            else:
                pl.when(jnp.logical_not(late[k]))(self.copies[k].start)

        go(0)
        go(1)
        self.packed[...] = pack_rows(self.tile[...], T // 2)
        go(2)
        go(3)
        d = self.d
        if d < T:
            self.plus[:, d:, :] = self.tile[:, : T - d, :]
            self.minus[:, : T - d, :] = self.tile[:, d:, :]
        if turn is not None:

            @pl.when(p.ends)
            def _():
                pl.semaphore_wait(turn, 4 - (p.inner & p.here).astype(jnp.int32))

            for k in range(4):
                pl.when(late[k])(self.copies[k].start)

    def arrive(self):
        for copy in self.copies:
            copy.wait_recv()
        d, h = self.d, T // 2
        self.plus[:h, :d, 128:] = self.got_plus[:, :, :64]
        self.plus[h:, :d, 128:] = self.got_plus[:, :, 64:]
        self.minus[:h, T - d :, 128:] = self.got_minus[:, :, :64]
        self.minus[h:, T - d :, 128:] = self.got_minus[:, :, 64:]

    def drain(self):
        for copy in self.copies:
            copy.wait_send()


def pack_columns(v):
    return jnp.concatenate([v[:, : T // 2, 128:], v[:, T // 2 :, 128:]], axis=-1)


class LatPair:
    def __init__(self, place, copies_north, copies_south):
        self.p, self.to_north, self.to_south = place, copies_north, copies_south

    def start(self):
        lat = self.p.lat

        @pl.when(lat == 2)
        def _():
            for copy in self.to_south:
                copy.start()

        @pl.when(self.p.has_north)
        def _():
            for copy in self.to_north:
                copy.start()

        @pl.when(self.p.has_south & (lat != 2))
        def _():
            for copy in self.to_south:
                copy.start()

    def arrive(self):
        @pl.when(self.p.has_south)
        def _():
            for copy in self.to_north:
                copy.wait_recv()

        @pl.when(self.p.has_north)
        def _():
            for copy in self.to_south:
                copy.wait_recv()

    def drain(self):
        @pl.when(self.p.has_north)
        def _():
            for copy in self.to_north:
                copy.wait_send()

        @pl.when(self.p.has_south)
        def _():
            for copy in self.to_south:
                copy.wait_send()


class Activation:
    def __init__(self, place, sems, wide, packed, got, turned, d):
        self.p, self.wide, self.packed, self.got, self.turned, self.d = place, wide, packed, got, turned, d
        lanes = pl.ds(0, 128)
        top, bottom = pl.ds(d, d), pl.ds(T, d)
        self.halo = LatPair(
            place,
            [
                remote(wide.at[bottom, :, lanes], wide.at[pl.ds(0, d), :, lanes], *sems.take(), place.north),
                remote(packed.at[pl.ds(T - d, d)], got.at[0], *sems.take(), place.north),
            ],
            [
                remote(wide.at[top, :, lanes], wide.at[pl.ds(T + d, d), :, lanes], *sems.take(), place.south),
                remote(packed.at[pl.ds(0, d)], got.at[1], *sems.take(), place.south),
            ],
        )

    def start(self):
        d = self.d

        @pl.loop(0, 4)
        def _(i):
            v = self.wide[pl.ds(d + i * 8, 8)]
            self.packed[pl.ds(i * 8, 8)] = pack_columns(v)

        self.halo.start()

        @pl.when(jnp.logical_not(self.p.has_south))
        def _():
            self.wide[:d] = jnp.zeros((d, T, C), BF)

        @pl.when(jnp.logical_not(self.p.has_north))
        def _():
            self.wide[T + d :] = jnp.zeros((d, T, C), BF)

    def arrive(self):
        d, h = self.d, T // 2
        self.halo.arrive()

        @pl.when(self.p.has_south)
        def _():
            self.wide[:d, :h, 128:] = self.got[0, :, :, :64]
            self.wide[:d, h:, 128:] = self.got[0, :, :, 64:]

        @pl.when(self.p.has_north)
        def _():
            self.wide[T + d :, :h, 128:] = self.got[1, :, :, :64]
            self.wide[T + d :, h:, 128:] = self.got[1, :, :, 64:]

        @pl.loop(0, (T + 2 * d) // 8)
        def _(i):
            v = self.wide[pl.ds(i * 8, 8)].reshape(8 * T, C)
            self.turned[:, pl.ds(pl.multiple_of(i * 8 * T, 8 * T), 8 * T)] = v.T

    def weight_gradient(self, minus, tile, plus, into):
        cells = T * T

        @pl.loop(0, 3)
        def _(r):
            start = pl.multiple_of(r * self.d * T, 512)
            turned = self.turned[:, pl.ds(start, cells)]
            for c, g in enumerate((minus, tile, plus)):
                d = jnp.dot(turned, g[...].reshape(cells, C), preferred_element_type=F32)
                base = pl.multiple_of((3 * r + c) * 288, 32)
                into[pl.ds(base, C)] = d[:, :128]
                into[pl.ds(base + C, C // 2)] = jnp.concatenate([d[: C // 2, 128:], d[C // 2 :, 128:]], axis=1)

        into[9 * 288 :] = jnp.zeros((ROWS - 9 * 288, 128), F32)


class Pull:
    def __init__(self, place, sems, minus, tile, plus, weights, wide_out, packed_out, wide_in, packed_in, total, d):
        self.p, self.g, self.w, self.d = place, (minus, tile, plus), weights, d
        self.wide_out, self.packed_out, self.wide_in, self.packed_in = wide_out, packed_out, wide_in, packed_in
        self.total = total
        self.halo = LatPair(
            place,
            [
                remote(wide_out.at[0], wide_in.at[0], *sems.take(), place.north),
                remote(packed_out.at[0], packed_in.at[0], *sems.take(), place.north),
            ],
            [
                remote(wide_out.at[1], wide_in.at[1], *sems.take(), place.south),
                remote(packed_out.at[1], packed_in.at[1], *sems.take(), place.south),
            ],
        )

    def partial(self, r, row):
        total = None
        for c in range(3):
            g = self.g[c][pl.ds(row, 8)].reshape(8 * T, C)
            term = lax.dot_general(
                g, self.w[3 * (r + 1) + c], (((1,), (1,)), ((), ())), preferred_element_type=F32
            )
            total = term if total is None else total + term
        return total.reshape(8, T, C)

    def send(self):
        d = self.d

        @pl.loop(0, d // 8)
        def _(i):
            for slot, r, first in ((0, 1, T - d), (1, -1, 0)):
                v = self.partial(r, first + i * 8).astype(BF)
                self.wide_out[slot, pl.ds(i * 8, 8)] = v[:, :, :128]
                self.packed_out[slot, pl.ds(i * 8, 8)] = pack_columns(v)

        self.halo.start()

        @pl.when(jnp.logical_not(self.p.has_south))
        def _():
            self.wide_in[0] = jnp.zeros(self.wide_in.shape[1:], BF)
            self.packed_in[0] = jnp.zeros(self.packed_in.shape[1:], BF)

        @pl.when(jnp.logical_not(self.p.has_north))
        def _():
            self.wide_in[1] = jnp.zeros(self.wide_in.shape[1:], BF)
            self.packed_in[1] = jnp.zeros(self.packed_in.shape[1:], BF)

    def stay(self):
        d = self.d

        @pl.loop(0, T // 8)
        def _(i):
            self.total[pl.ds(i * 8, 8)] = self.partial(0, i * 8)

        if d < T:

            @pl.loop(0, (T - d) // 8)
            def _(i):
                self.total[pl.ds(d + i * 8, 8)] += self.partial(1, i * 8)
                self.total[pl.ds(i * 8, 8)] += self.partial(-1, d + i * 8)

    def finish(self, use, turn=None):
        d = self.d
        self.halo.arrive()
        self.halo.drain()
        if turn is not None:

            self.p.column_first(
                lambda where: pl.semaphore_signal(turn, inc=1, device_id=where, device_id_type=MESH), None
            )

        def got(slot, row):
            w = self.wide_in[slot, pl.ds(row, 8)].astype(F32)
            q = self.packed_in[slot, pl.ds(row, 8)].astype(F32)
            return jnp.concatenate([w, jnp.concatenate([q[:, :, :64], q[:, :, 64:]], axis=1)], axis=-1)

        if d == T:

            @pl.loop(0, T // 8)
            def _(i):
                use(i * 8, self.total[pl.ds(i * 8, 8)] + got(0, i * 8) + got(1, i * 8))

        else:

            @pl.loop(0, d // 8)
            def _(i):
                use(i * 8, self.total[pl.ds(i * 8, 8)] + got(0, i * 8))
                use(T - d + i * 8, self.total[pl.ds(T - d + i * 8, 8)] + got(1, i * 8))


def scratch():
    v = pltpu.VMEM
    shapes = {}
    for b, d in (("1", DILATION_FIRST), ("2", DILATION_SECOND)):
        shapes["a" + b] = v((T, T, C), BF)
        shapes["slope" + b] = v((T, T, C), F32)
        for n in ("w1", "w2"):
            shapes[n + b] = v((9, C, C), BF)
        for n in ("h", "x"):
            shapes[n + b] = v((T + 2 * d, T, C), BF)
            shapes[n + b + "packed"] = v((T, T // 2, 128), BF)
            shapes[n + b + "got"] = v((2, d, T // 2, 128), BF)
            shapes[n + b + "turned"] = v((C, (T + 2 * d) * T), BF)
        for n in ("g", "q"):
            shapes[n + b] = v((T, T, C), BF)
            shapes[n + b + "packed"] = v((T // 2, T, 128), BF)
            for s in ("plus", "minus"):
                shapes[n + b + s] = v((T, T, C), BF)
                shapes[n + b + "got_" + s] = v((T // 2, d, 128), BF)
            for s in ("wide_out", "wide_in"):
                shapes[n + b + s] = v((2, d, T, 128), BF)
            for s in ("packed_out", "packed_in"):
                shapes[n + b + s] = v((2, d, T // 2, 128), BF)
        for n in ("1", "2"):
            m = "r" + n + b
            shapes[m + "local"] = v((ROWS, 128), F32)
            shapes[m + "from_twin"] = v((HALF, 128), F32)
            shapes[m + "xs"] = v((HALF, 128), BF)
            shapes[m + "xr"] = v((3, QUART, 128), BF)
            shapes[m + "zs"] = v((QUART, 128), BF)
            shapes[m + "zr"] = v((7, SHARD, 128), BF)
            shapes[m + "yr"] = v((4, SHARD, 128), F32)
            shapes[m + "out"] = v((ROWS, 128), BF)
    shapes["total"] = v((T, T, C), F32)
    shapes["dx"] = v((T, T, C), BF)
    shapes["load"] = pltpu.SemaphoreType.DMA((9,))
    shapes["store"] = pltpu.SemaphoreType.DMA((5,))
    shapes["send"] = pltpu.SemaphoreType.DMA((160,))
    shapes["turn"] = pltpu.SemaphoreType.REGULAR((3,))
    shapes["recv"] = pltpu.SemaphoreType.DMA((160,))
    return shapes


NAMES = tuple(scratch())


def body(x1, a1, x2, a2, g2, w11, w21, w12, w22, dx_out, r11_out, r21_out, r12_out, r22_out, *refs):
    s = dict(zip(NAMES, refs))
    p = Place()
    loads = {}
    d1, d2 = DILATION_FIRST, DILATION_SECOND
    for k, (name, src, dst) in enumerate(
        (
            ("g2", g2, s["g2"]),
            ("a2", a2, s["a2"]),
            ("x2", x2, s["x2"].at[pl.ds(d2, T)]),
            ("w22", w22, s["w22"]),
            ("a1", a1, s["a1"]),
            ("x1", x1, s["x1"].at[pl.ds(d1, T)]),
            ("w12", w12, s["w12"]),
            ("w21", w21, s["w21"]),
            ("w11", w11, s["w11"]),
        )
    ):
        loads[name] = pltpu.make_async_copy(src, dst, s["load"].at[k])
        loads[name].start()

    barrier = pltpu.get_barrier_semaphore()
    peers = [p.east, p.west, p.twin]
    peers += [p.at_x(k)[1] for k in range(1, 4)] + [p.at_y(k)[1] for k in range(1, 4)]
    peers += [p.at_z(k)[1] for k in range(1, 8)]
    for where in peers:
        pl.semaphore_signal(barrier, inc=1, device_id=where, device_id_type=MESH)
    for cond, where in ((p.has_north, p.north), (p.has_south, p.south)):

        @pl.when(cond)
        def _():
            pl.semaphore_signal(barrier, inc=1, device_id=where, device_id_type=MESH)

    def greet(where):
        pl.semaphore_signal(barrier, inc=1, device_id=where, device_id_type=MESH)

    p.column_first(greet, greet)
    expected = len(peers) + p.has_north.astype(jnp.int32) + p.has_south.astype(jnp.int32)
    mine = (p.here & p.inner).astype(jnp.int32)
    expected += p.ends.astype(jnp.int32) * (4 - mine)
    expected += (p.ends & p.inner).astype(jnp.int32) * (8 - p.here.astype(jnp.int32))

    sems = Sems(s["send"], s["recv"])

    def reduction(m):
        names = ("local", "from_twin", "xs", "xr", "zs", "zr", "yr", "out")
        return Reduction(p, sems, *(s[m + n] for n in names))

    def lon_halo(m, d):
        names = ("", "packed", "plus", "minus", "got_plus", "got_minus")
        return LonHalo(p, sems, *(s[m + n] for n in names), d)

    def pull(m, w, d):
        names = ("minus", "", "plus")
        outs = ("wide_out", "packed_out", "wide_in", "packed_in")
        return Pull(p, sems, *(s[m + n] for n in names), s[w], *(s[m + n] for n in outs), s["total"], d)

    def activation(m, d):
        return Activation(p, sems, *(s[m + n] for n in ("", "packed", "got", "turned")), d)

    red = {m: reduction(m) for m in ("r22", "r12", "r21", "r11")}
    halos = {m: lon_halo(m, d) for m, d in (("g2", d2), ("q2", d2), ("g1", d1), ("q1", d1))}
    pulls = {
        m: pull(m, w, d) for m, w, d in (("g2", "w22", d2), ("q2", "w12", d2), ("g1", "w21", d1), ("q1", "w11", d1))
    }
    acts = {m: activation(m, d) for m, d in (("h2", d2), ("x2", d2), ("h1", d1), ("x1", d1))}

    def gate(b, d):
        @pl.loop(0, T // 4)
        def _(i):
            rows = pl.ds(i * 4, 4)
            pre = s["a" + b][rows].astype(F32)
            sigma = jax.nn.sigmoid(pre)
            s["h" + b][pl.ds(d + i * 4, 4)] = (pre * sigma).astype(BF)
            s["slope" + b][rows] = sigma * (1.0 + pre * (1.0 - sigma))

    def use_pre(b):
        def use(row, v):
            s["q" + b][pl.ds(row, 8)] = (v * s["slope" + b][pl.ds(row, 8)]).astype(BF)

        return use

    def use_x(b, into):
        def use(row, v):
            into[pl.ds(row, 8)] = (s["g" + b][pl.ds(row, 8)].astype(F32) + v).astype(BF)

        return use

    def weight(act, m, r):
        acts[act].weight_gradient(s[m + "minus"], s[m], s[m + "plus"], s[r + "local"])

    loads["g2"].wait()
    pl.semaphore_wait(barrier, expected)
    halos["g2"].start()
    loads["a2"].wait()
    gate("2", d2)
    loads["a1"].wait()
    gate("1", d1)
    loads["x1"].wait()
    loads["x2"].wait()
    for name in ("w22", "w12", "w21", "w11"):
        loads[name].wait()

    turns = [s["turn"].at[k] for k in range(3)]

    halos["g2"].drain()
    acts["h2"].start()
    halos["g2"].arrive()
    pulls["g2"].send()
    pulls["g2"].stay()
    pulls["g2"].finish(use_pre("2"), turns[0])
    halos["q2"].start(turns[0])
    acts["h2"].arrive()
    weight("h2", "g2", "r22")
    red["r22"].go()
    halos["q2"].drain()
    acts["x2"].start()

    halos["q2"].arrive()
    pulls["q2"].send()
    pulls["q2"].stay()
    red["r22"].go()
    pulls["q2"].finish(use_x("2", s["g1"]), turns[1])
    halos["g1"].start(turns[1])
    acts["x2"].arrive()
    weight("x2", "q2", "r12")
    red["r12"].go()
    halos["g1"].drain()
    acts["x1"].start()
    acts["h1"].start()
    red["r22"].go()

    halos["g1"].arrive()
    pulls["g1"].send()
    pulls["g1"].stay()
    red["r12"].go()
    pulls["g1"].finish(use_pre("1"), turns[2])
    halos["q1"].start(turns[2])
    acts["h1"].arrive()
    weight("h1", "g1", "r21")
    red["r21"].go()
    acts["x1"].arrive()
    red["r22"].go()
    red["r12"].go()
    red["r21"].go()

    halos["q1"].arrive()
    weight("x1", "q1", "r11")
    red["r11"].go()
    pulls["q1"].send()
    pulls["q1"].stay()
    red["r11"].go()
    red["r22"].go()
    red["r12"].go()
    red["r21"].go()
    pulls["q1"].finish(use_x("1", s["dx"]))
    stores = [pltpu.make_async_copy(s["dx"], dx_out, s["store"].at[0])]
    stores[0].start()
    red["r11"].go()
    red["r12"].go()
    red["r22"].go()
    red["r21"].go()
    red["r11"].go()
    red["r12"].go()
    red["r22"].go()
    red["r21"].go()
    red["r11"].go()
    red["r12"].go()
    red["r21"].go()
    red["r11"].go()
    red["r12"].go()
    red["r21"].go()
    red["r11"].go()
    red["r21"].go()
    red["r22"].go()
    red["r11"].go()
    for k, (m, out) in enumerate((("r22", r22_out), ("r12", r12_out), ("r21", r21_out), ("r11", r11_out))):
        stores.append(pltpu.make_async_copy(s[m + "out"], out, s["store"].at[1 + k]))
        stores[-1].start()
    halos["q1"].drain()
    assert all(part.step == 8 for part in red.values())
    for part in red.values():
        part.drain()
    for part in acts.values():
        part.halo.drain()
    for copy in stores:
        copy.wait()


def unpack(*refs):
    tile_in, *sums_in = refs[:5]
    tile_out, *sums_out = refs[5:10]
    tile, *buffers = refs[10:19]
    took, gave = refs[19:]
    reads = [pltpu.make_async_copy(a, b, took.at[k]) for k, (a, b) in enumerate(zip(sums_in, buffers[:4]))]
    reads.append(pltpu.make_async_copy(tile_in, tile, took.at[4]))
    writes = [pltpu.make_async_copy(a, b, gave.at[k]) for k, (a, b) in enumerate(zip(buffers[4:], sums_out))]
    writes.append(pltpu.make_async_copy(tile, tile_out, gave.at[4]))
    for copy in reads:
        copy.start()
    for k in range(4):
        reads[k].wait()

        @pl.loop(0, 9)
        def _(tap):
            base = pl.multiple_of(tap * 288, 32)
            wide = buffers[k][pl.ds(base, C)].astype(F32)
            rest = buffers[k][pl.ds(base + C, C // 2)].astype(F32)
            buffers[4 + k][tap, :, :128] = wide
            buffers[4 + k][tap, : C // 2, 128:] = rest[:, :64]
            buffers[4 + k][tap, C // 2 :, 128:] = rest[:, 64:]

        writes[k].start()
    reads[4].wait()
    writes[4].start()
    for copy in writes:
        copy.wait()


def local(x1, a1, x2, a2, g2, w11, w21, w12, w22):
    shapes = scratch()
    anywhere = pl.BlockSpec(memory_space=pl.ANY)
    packed = jax.ShapeDtypeStruct((ROWS, 128), BF)
    dx, *sums = pl.pallas_call(
        body,
        name="backward",
        out_shape=(jax.ShapeDtypeStruct((T, T, C), BF), packed, packed, packed, packed),
        in_specs=[anywhere] * 9,
        out_specs=[anywhere] * 5,
        scratch_shapes=list(shapes.values()),
        compiler_params=pltpu.CompilerParams(
            collective_id=0, has_side_effects=True, vmem_limit_bytes=60 * 1024 * 1024
        ),
    )(x1, a1, x2, a2, g2, w11, w21, w12, w22)
    full = jax.ShapeDtypeStruct((9, C, C), F32)
    return pl.pallas_call(
        unpack,
        name="unpack",
        out_shape=(jax.ShapeDtypeStruct((T, T, C), BF), full, full, full, full),
        in_specs=[anywhere] * 5,
        out_specs=[anywhere] * 5,
        scratch_shapes=[pltpu.VMEM((T, T, C), BF)]
        + [pltpu.VMEM((ROWS, 128), BF)] * 4
        + [pltpu.VMEM((9, C, C), F32)] * 4
        + [pltpu.SemaphoreType.DMA((5,)), pltpu.SemaphoreType.DMA((5,))],
    )(dx, *sums)


def solution(mesh):
    tile = P("lat", "lon", None)
    return jax.shard_map(
        local,
        mesh=mesh,
        in_specs=(tile,) * 5 + (P(),) * 4,
        out_specs=(tile, P(), P(), P(), P()),
        check_vma=False,
    )
```

```python
import jax
import jax.numpy as jnp
from jax import lax
from jax.experimental import pallas as pl
from jax.experimental.pallas import tpu as pltpu
from jax.sharding import PartitionSpec as P

C = 192
DILATION_FIRST = 16
DILATION_SECOND = 32
MESH = pl.DeviceIdType.MESH
BF = jnp.bfloat16
F32 = jnp.float32
T = 32
ROWS = 3072
HALF, QUART, PART, SHARD = ROWS // 2, ROWS // 8, ROWS // 32, ROWS // 64


class Place:
    def __init__(self):
        lon, lat = lax.axis_index("lon"), lax.axis_index("lat")
        self.lon, self.lat = lon, lat
        self.x, self.yh, self.z = lon // 16, (lon // 8) % 2, lon % 8
        self.yl, self.core = lat // 2, lat % 2
        self.y = self.yh * 2 + self.yl
        self.east = {"lon": (lon + 1) % 64, "lat": lat}
        self.west = {"lon": (lon + 63) % 64, "lat": lat}
        self.north = {"lon": lon, "lat": jnp.minimum(lat + 1, 3)}
        self.south = {"lon": lon, "lat": jnp.maximum(lat - 1, 0)}
        self.twin = {"lon": lon, "lat": lat + 1 - 2 * self.core}
        self.has_north, self.has_south = lat < 3, lat > 0
        self.ends = (self.z == 0) | (self.z == 7)
        self.inner = (lat == 1) | (lat == 2)
        top = (self.z == 7).astype(jnp.int32)
        half = 1 - top
        self.here = self.yh == half
        away = 2 * top - 1
        beside = (self.x + 4 + away) % 4
        self.column = jnp.where(self.here, self.x, beside)
        self.senders = (self.x * 16 + half * 8 + self.z, ((self.x + 4 - away) % 4) * 16 + top * 8 + self.z)

    def column_first(self, to_senders, to_column):
        @pl.when(self.ends & self.inner)
        def _():
            for k, lon in enumerate(self.senders):
                for lat in range(4):
                    other = jnp.logical_not(self.here & (self.lat == lat)) if k == 0 else self.ends
                    pl.when(other)(lambda lon=lon, lat=lat: to_senders({"lon": lon, "lat": lat}))

        if to_column is not None:

            @pl.when(self.ends)
            def _():
                for yh in range(2):
                    for lat in (1, 2):
                        other = jnp.logical_not(self.here & (self.yh == yh) & (self.lat == lat))
                        lon = self.column * 16 + yh * 8 + self.z
                        pl.when(other)(lambda lon=lon, lat=lat: to_column({"lon": lon, "lat": lat}))

    def at_x(self, k):
        x = (self.x + k) % 4
        return x, {"lon": x * 16 + self.lon % 16, "lat": self.lat}

    def at_y(self, k):
        y = (self.y + k) % 4
        return y, {"lon": self.x * 16 + (y // 2) * 8 + self.z, "lat": (y % 2) * 2 + self.core}

    def at_xy(self, k):
        x, y = (self.x + k // 4) % 4, (self.y + k % 4) % 4
        return x * 4 + y, {"lon": x * 16 + (y // 2) * 8 + self.z, "lat": (y % 2) * 2 + self.core}

    def at_z(self, k):
        z = (self.z + k) % 8
        return z, {"lon": self.lon - self.z + z, "lat": self.lat}


def remote(src, dst, send, recv, where):
    return pltpu.make_async_remote_copy(
        src_ref=src, dst_ref=dst, send_sem=send, recv_sem=recv, device_id=where, device_id_type=MESH
    )


class Sems:
    def __init__(self, send, recv):
        self.send, self.recv, self.n = send, recv, 0

    def take(self):
        k = self.n
        self.n += 1
        return self.send.at[k], self.recv.at[k]


class Reduction:
    def __init__(self, place, sems, along_x, local, from_twin, xs, xr, zs, zr, yr, out):
        self.p, self.local, self.from_twin = place, local, from_twin
        self.xs, self.xr, self.zs, self.zr, self.yr, self.out = xs, xr, zs, zr, yr, out
        p = place
        self.wide, at_wide = (p.x, p.at_x) if along_x else (p.y, p.at_y)
        thin, at_thin = (p.y, p.at_y) if along_x else (p.x, p.at_x)
        self.thin = thin
        self.mine = pl.multiple_of(p.core * HALF, HALF)
        other = pl.multiple_of((1 - p.core) * HALF, HALF)
        quarter = pl.multiple_of(self.mine + self.wide * QUART, QUART)
        self.shard = pl.ds(pl.multiple_of(quarter + p.z * SHARD, SHARD), SHARD)
        self.twin = [remote(local.at[pl.ds(other, HALF)], from_twin, *sems.take(), p.twin)]
        self.to_x = []
        for k in range(1, 4):
            x, where = at_wide(k)
            src = xs.at[pl.ds(pl.multiple_of(x * QUART, QUART), QUART)]
            self.to_x.append(remote(src, xr.at[k - 1], *sems.take(), where))
        self.to_z = []
        for k in range(1, 8):
            z, where = p.at_z(k)
            src = zs.at[pl.ds(pl.multiple_of(z * SHARD, SHARD), SHARD)]
            self.to_z.append(remote(src, zr.at[k - 1], *sems.take(), where))
        self.to_y = [remote(yr.at[thin], yr.at[thin], *sems.take(), at_thin(k)[1]) for k in range(1, 4)]
        ref = out.at[self.shard]
        self.all_z = [remote(ref, ref, *sems.take(), p.at_z(k)[1]) for k in range(1, 8)]
        ref = out.at[pl.ds(quarter, QUART)]
        self.all_x = [remote(ref, ref, *sems.take(), at_wide(k)[1]) for k in range(1, 4)]
        self.all_twin = []
        for k in range(4):
            ref = out.at[pl.ds(pl.multiple_of(self.mine + ((self.wide + 4 - k) % 4) * QUART, QUART), QUART)]
            self.all_twin.append(remote(ref, ref, *sems.take(), p.twin))
        self.step = 0

    def go(self):
        getattr(self, f"step{self.step}")()
        self.step += 1

    def start(self, copies):
        for copy in copies:
            copy.start()

    def arrive(self, copies):
        for copy in copies:
            copy.wait_recv()

    def step0(self):
        self.start(self.twin)

    def step1(self):
        self.arrive(self.twin)

        @pl.loop(0, HALF // 128)
        def _(i):
            rows = pl.ds(pl.multiple_of(i * 128, 128), 128)
            own = self.local[pl.ds(pl.multiple_of(self.mine + i * 128, 128), 128)]
            self.xs[rows] = (own + self.from_twin[rows]).astype(BF)

        self.start(self.to_x)

    def step2(self):
        self.arrive(self.to_x)
        total = self.xs[pl.ds(pl.multiple_of(self.wide * QUART, QUART), QUART)].astype(F32)
        for k in range(3):
            total = total + self.xr[k].astype(F32)
        self.zs[...] = total.astype(BF)
        self.start(self.to_z)

    def step3(self):
        self.arrive(self.to_z)
        total = self.zs[pl.ds(pl.multiple_of(self.p.z * SHARD, SHARD), SHARD)].astype(F32)
        for k in range(7):
            total = total + self.zr[k].astype(F32)
        self.yr[self.thin] = total
        self.start(self.to_y)

    def step4(self):
        self.arrive(self.to_y)
        self.out[self.shard] = ((self.yr[0] + self.yr[1]) + (self.yr[2] + self.yr[3])).astype(BF)
        self.start(self.all_z)

    def step5(self):
        self.arrive(self.all_z)
        self.start(self.all_x)
        self.all_twin[0].start()

    def step6(self):
        for k in range(3):
            self.all_x[k].wait_recv()
            self.all_twin[k + 1].start()

    def step7(self):
        self.arrive(self.all_twin)

    def drain(self):
        for copies in (self.twin, self.to_x, self.to_z, self.to_y, self.all_z, self.all_x, self.all_twin):
            for copy in copies:
                copy.wait_send()


class LastReduction(Reduction):
    def __init__(self, place, sems, local, from_twin, xs, xr, zs, zr, out):
        self.p, self.local, self.from_twin = place, local, from_twin
        self.xs, self.xr, self.zs, self.zr, self.out = xs, xr, zs, zr, out
        p = place
        self.mine = pl.multiple_of(p.core * HALF, HALF)
        other = pl.multiple_of((1 - p.core) * HALF, HALF)
        self.own = pl.multiple_of((p.x * 4 + p.y) * PART, PART)
        self.twin = [remote(local.at[pl.ds(other, HALF)], from_twin, *sems.take(), p.twin)]
        self.to_x = []
        for k in range(1, 16):
            xy, where = p.at_xy(k)
            src = xs.at[pl.ds(pl.multiple_of(xy * PART, PART), PART)]
            self.to_x.append(remote(src, xr.at[k - 1], *sems.take(), where))
        self.to_z = [remote(zs, zr.at[p.z], *sems.take(), p.at_z(k)[1]) for k in range(1, 8)]
        self.to_y = []
        self.shard = pl.ds(pl.multiple_of(self.mine + self.own, PART), PART)
        ref = out.at[self.shard]
        self.all_z = [remote(ref, ref, *sems.take(), p.at_xy(k)[1]) for k in range(1, 16)]
        self.all_x = []
        ref = out.at[pl.ds(self.mine, HALF)]
        self.all_twin = [remote(ref, ref, *sems.take(), p.twin)]
        self.step = 0

    def step2(self):
        self.arrive(self.to_x)
        total = self.xs[pl.ds(self.own, PART)].astype(F32)
        for k in range(15):
            total = total + self.xr[k].astype(F32)
        total = total.astype(BF)
        self.zs[...] = total
        self.zr[self.p.z] = total
        self.start(self.to_z)

    def step3(self):
        self.arrive(self.to_z)
        total = self.zr[0].astype(F32)
        for k in range(1, 8):
            total = total + self.zr[k].astype(F32)
        self.out[self.shard] = total.astype(BF)
        self.start(self.all_z)

    def step4(self):
        self.arrive(self.all_z)
        self.start(self.all_twin)

    def step5(self):
        self.arrive(self.all_twin)


def pack_rows(v, half):
    return jnp.concatenate([v[:half, :, 128:], v[half:, :, 128:]], axis=-1)


class LonHalo:
    def __init__(self, place, sems, tile, packed, plus, minus, got_plus, got_minus, d):
        self.p = place
        self.tile, self.packed, self.plus, self.minus, self.d = tile, packed, plus, minus, d
        self.got_plus, self.got_minus = got_plus, got_minus
        low, high = pl.ds(0, d), pl.ds(T - d, d)
        wide = pl.ds(0, 128)
        self.copies = [
            remote(tile.at[:, high, wide], plus.at[:, low, wide], *sems.take(), place.east),
            remote(tile.at[:, low, wide], minus.at[:, high, wide], *sems.take(), place.west),
            remote(packed.at[:, high], got_plus, *sems.take(), place.east),
            remote(packed.at[:, low], got_minus, *sems.take(), place.west),
        ]

    def start(self, turn=None):
        p = self.p
        late = [(p.z == z) if turn is not None else None for z in (7, 0, 7, 0)]

        def go(k):
            if late[k] is None:
                self.copies[k].start()
            else:
                pl.when(jnp.logical_not(late[k]))(self.copies[k].start)

        go(0)
        go(1)
        self.packed[...] = pack_rows(self.tile[...], T // 2)
        go(2)
        go(3)
        d = self.d
        if d < T:
            self.plus[:, d:, :] = self.tile[:, : T - d, :]
            self.minus[:, : T - d, :] = self.tile[:, d:, :]
        if turn is not None:

            @pl.when(p.ends)
            def _():
                pl.semaphore_wait(turn, 4 - (p.inner & p.here).astype(jnp.int32))

            for k in range(4):
                pl.when(late[k])(self.copies[k].start)

    def arrive(self):
        for copy in self.copies:
            copy.wait_recv()
        d, h = self.d, T // 2
        self.plus[:h, :d, 128:] = self.got_plus[:, :, :64]
        self.plus[h:, :d, 128:] = self.got_plus[:, :, 64:]
        self.minus[:h, T - d :, 128:] = self.got_minus[:, :, :64]
        self.minus[h:, T - d :, 128:] = self.got_minus[:, :, 64:]

    def drain(self):
        for copy in self.copies:
            copy.wait_send()


def pack_columns(v):
    return jnp.concatenate([v[:, : T // 2, 128:], v[:, T // 2 :, 128:]], axis=-1)


class LatPair:
    def __init__(self, place, copies_north, copies_south):
        self.p, self.to_north, self.to_south = place, copies_north, copies_south

    def start(self):
        lat = self.p.lat

        @pl.when(lat == 2)
        def _():
            for copy in self.to_south:
                copy.start()

        @pl.when(self.p.has_north)
        def _():
            for copy in self.to_north:
                copy.start()

        @pl.when(self.p.has_south & (lat != 2))
        def _():
            for copy in self.to_south:
                copy.start()

    def arrive(self):
        @pl.when(self.p.has_south)
        def _():
            for copy in self.to_north:
                copy.wait_recv()

        @pl.when(self.p.has_north)
        def _():
            for copy in self.to_south:
                copy.wait_recv()

    def drain(self):
        @pl.when(self.p.has_north)
        def _():
            for copy in self.to_north:
                copy.wait_send()

        @pl.when(self.p.has_south)
        def _():
            for copy in self.to_south:
                copy.wait_send()


class Activation:
    def __init__(self, place, sems, wide, packed, got, turned, d):
        self.p, self.wide, self.packed, self.got, self.turned, self.d = place, wide, packed, got, turned, d
        lanes = pl.ds(0, 128)
        top, bottom = pl.ds(d, d), pl.ds(T, d)
        self.halo = LatPair(
            place,
            [
                remote(wide.at[bottom, :, lanes], wide.at[pl.ds(0, d), :, lanes], *sems.take(), place.north),
                remote(packed.at[pl.ds(T - d, d)], got.at[0], *sems.take(), place.north),
            ],
            [
                remote(wide.at[top, :, lanes], wide.at[pl.ds(T + d, d), :, lanes], *sems.take(), place.south),
                remote(packed.at[pl.ds(0, d)], got.at[1], *sems.take(), place.south),
            ],
        )

    def start(self):
        d = self.d

        @pl.loop(0, 4)
        def _(i):
            v = self.wide[pl.ds(d + i * 8, 8)]
            self.packed[pl.ds(i * 8, 8)] = pack_columns(v)

        self.halo.start()

        @pl.when(jnp.logical_not(self.p.has_south))
        def _():
            self.wide[:d] = jnp.zeros((d, T, C), BF)

        @pl.when(jnp.logical_not(self.p.has_north))
        def _():
            self.wide[T + d :] = jnp.zeros((d, T, C), BF)

    def arrive(self):
        d, h = self.d, T // 2
        self.halo.arrive()

        @pl.when(self.p.has_south)
        def _():
            self.wide[:d, :h, 128:] = self.got[0, :, :, :64]
            self.wide[:d, h:, 128:] = self.got[0, :, :, 64:]

        @pl.when(self.p.has_north)
        def _():
            self.wide[T + d :, :h, 128:] = self.got[1, :, :, :64]
            self.wide[T + d :, h:, 128:] = self.got[1, :, :, 64:]

        @pl.loop(0, (T + 2 * d) // 8)
        def _(i):
            v = self.wide[pl.ds(i * 8, 8)].reshape(8 * T, C)
            self.turned[:, pl.ds(pl.multiple_of(i * 8 * T, 8 * T), 8 * T)] = v.T

    def weight_gradient(self, gradients, into):
        cells = T * T

        @pl.loop(0, 3)
        def _(r):
            start = pl.multiple_of(r * self.d * T, 512)
            turned = self.turned[:, pl.ds(start, cells)]
            for c, g in gradients:
                d = jnp.dot(turned, g[...].reshape(cells, C), preferred_element_type=F32)
                base = pl.multiple_of((3 * r + c) * 288, 32)
                into[pl.ds(base, C)] = d[:, :128]
                into[pl.ds(base + C, C // 2)] = jnp.concatenate([d[: C // 2, 128:], d[C // 2 :, 128:]], axis=1)


class Pull:
    def __init__(self, place, sems, minus, tile, plus, weights, wide_out, packed_out, wide_in, packed_in, total, d):
        self.p, self.g, self.w, self.d = place, (minus, tile, plus), weights, d
        self.wide_out, self.packed_out, self.wide_in, self.packed_in = wide_out, packed_out, wide_in, packed_in
        self.total = total
        self.halo = LatPair(
            place,
            [
                remote(wide_out.at[0], wide_in.at[0], *sems.take(), place.north),
                remote(packed_out.at[0], packed_in.at[0], *sems.take(), place.north),
            ],
            [
                remote(wide_out.at[1], wide_in.at[1], *sems.take(), place.south),
                remote(packed_out.at[1], packed_in.at[1], *sems.take(), place.south),
            ],
        )

    def partial(self, r, row, rows=8):
        total = None
        for c in range(3):
            g = self.g[c][pl.ds(row, rows)].reshape(rows * T, C)
            term = lax.dot_general(
                g, self.w[3 * (r + 1) + c], (((1,), (1,)), ((), ())), preferred_element_type=F32
            )
            total = term if total is None else total + term
        return total.reshape(rows, T, C)

    def send(self):
        d, p = self.d, self.p
        slots = ((p.has_north, 1, T - d, self.halo.to_north), (p.has_south, -1, 0, self.halo.to_south))
        for core, order in ((1, (0, 1)), (0, (1, 0))):
            for slot in order:
                there, r, first, copies = slots[slot]

                @pl.when((p.core == core) & there)
                def _(slot=slot, r=r, first=first, copies=copies):
                    @pl.loop(0, d // 16)
                    def _(i):
                        v = self.partial(r, first + i * 16, 16).astype(BF)
                        self.wide_out[slot, pl.ds(i * 16, 16)] = v[:, :, :128]
                        self.packed_out[slot, pl.ds(i * 16, 16)] = pack_columns(v)

                    for copy in copies:
                        copy.start()

        @pl.when(jnp.logical_not(self.p.has_south))
        def _():
            self.wide_in[0] = jnp.zeros(self.wide_in.shape[1:], BF)
            self.packed_in[0] = jnp.zeros(self.packed_in.shape[1:], BF)

        @pl.when(jnp.logical_not(self.p.has_north))
        def _():
            self.wide_in[1] = jnp.zeros(self.wide_in.shape[1:], BF)
            self.packed_in[1] = jnp.zeros(self.packed_in.shape[1:], BF)

    def stay(self):
        d = self.d

        @pl.loop(0, T // 8)
        def _(i):
            self.total[pl.ds(i * 8, 8)] = self.partial(0, i * 8)

        if d < T:

            @pl.loop(0, (T - d) // 8)
            def _(i):
                self.total[pl.ds(d + i * 8, 8)] += self.partial(1, i * 8)
                self.total[pl.ds(i * 8, 8)] += self.partial(-1, d + i * 8)

    def finish(self, use, turn=None):
        d = self.d
        self.halo.drain()
        if turn is not None:

            self.p.column_first(
                lambda where: pl.semaphore_signal(turn, inc=1, device_id=where, device_id_type=MESH), None
            )
        self.halo.arrive()

        def got(slot, row):
            w = self.wide_in[slot, pl.ds(row, 8)].astype(F32)
            q = self.packed_in[slot, pl.ds(row, 8)].astype(F32)
            return jnp.concatenate([w, jnp.concatenate([q[:, :, :64], q[:, :, 64:]], axis=1)], axis=-1)

        if d == T:

            @pl.loop(0, T // 8)
            def _(i):
                use(i * 8, self.total[pl.ds(i * 8, 8)] + got(0, i * 8) + got(1, i * 8))

        else:

            @pl.loop(0, d // 8)
            def _(i):
                use(i * 8, self.total[pl.ds(i * 8, 8)] + got(0, i * 8))
                use(T - d + i * 8, self.total[pl.ds(T - d + i * 8, 8)] + got(1, i * 8))


def scratch():
    v = pltpu.VMEM
    shapes = {}
    for b, d in (("1", DILATION_FIRST), ("2", DILATION_SECOND)):
        shapes["a" + b] = v((T, T, C), BF)
        shapes["slope" + b] = v((T, T, C), F32)
        for n in ("w1", "w2"):
            shapes[n + b] = v((9, C, C), BF)
        for n in ("h", "x"):
            shapes[n + b] = v((T + 2 * d, T, C), BF)
            shapes[n + b + "packed"] = v((T, T // 2, 128), BF)
            shapes[n + b + "got"] = v((2, d, T // 2, 128), BF)
            shapes[n + b + "turned"] = v((C, (T + 2 * d) * T), BF)
        for n in ("g", "q"):
            shapes[n + b] = v((T, T, C), BF)
            shapes[n + b + "packed"] = v((T // 2, T, 128), BF)
            for s in ("plus", "minus"):
                shapes[n + b + s] = v((T, T, C), BF)
                shapes[n + b + "got_" + s] = v((T // 2, d, 128), BF)
            for s in ("wide_out", "wide_in"):
                shapes[n + b + s] = v((2, d, T, 128), BF)
            for s in ("packed_out", "packed_in"):
                shapes[n + b + s] = v((2, d, T // 2, 128), BF)
        for n in ("1", "2"):
            m = "r" + n + b
            shapes[m + "local"] = v((ROWS, 128), F32)
            shapes[m + "from_twin"] = v((HALF, 128), F32)
            last = m == "r11"
            shapes[m + "xs"] = v((HALF, 128), BF)
            shapes[m + "xr"] = v((15, PART, 128) if last else (3, QUART, 128), BF)
            shapes[m + "zs"] = v((PART if last else QUART, 128), BF)
            shapes[m + "zr"] = v((8, PART, 128) if last else (7, SHARD, 128), BF)
            if not last:
                shapes[m + "yr"] = v((4, SHARD, 128), F32)
            shapes[m + "out"] = v((ROWS, 128), BF)
    shapes["total"] = v((T, T, C), F32)
    shapes["dx"] = v((T, T, C), BF)
    shapes["load"] = pltpu.SemaphoreType.DMA((9,))
    shapes["store"] = pltpu.SemaphoreType.DMA((5,))
    shapes["send"] = pltpu.SemaphoreType.DMA((192,))
    shapes["turn"] = pltpu.SemaphoreType.REGULAR((3,))
    shapes["recv"] = pltpu.SemaphoreType.DMA((192,))
    return shapes


NAMES = tuple(scratch())


def body(x1, a1, x2, a2, g2, w11, w21, w12, w22, dx_out, r11_out, r21_out, r12_out, r22_out, *refs):
    s = dict(zip(NAMES, refs))
    p = Place()
    loads = {}
    d1, d2 = DILATION_FIRST, DILATION_SECOND
    for k, (name, src, dst) in enumerate(
        (
            ("g2", g2, s["g2"]),
            ("a2", a2, s["a2"]),
            ("x2", x2, s["x2"].at[pl.ds(d2, T)]),
            ("w22", w22, s["w22"]),
            ("a1", a1, s["a1"]),
            ("x1", x1, s["x1"].at[pl.ds(d1, T)]),
            ("w12", w12, s["w12"]),
            ("w21", w21, s["w21"]),
            ("w11", w11, s["w11"]),
        )
    ):
        loads[name] = pltpu.make_async_copy(src, dst, s["load"].at[k])
        loads[name].start()

    barrier = pltpu.get_barrier_semaphore()
    peers = [p.east, p.west, p.twin]
    peers += [p.at_xy(k)[1] for k in range(1, 16)]
    peers += [p.at_z(k)[1] for k in range(1, 8)]
    for where in peers:
        pl.semaphore_signal(barrier, inc=1, device_id=where, device_id_type=MESH)
    for cond, where in ((p.has_north, p.north), (p.has_south, p.south)):

        @pl.when(cond)
        def _():
            pl.semaphore_signal(barrier, inc=1, device_id=where, device_id_type=MESH)

    def greet(where):
        pl.semaphore_signal(barrier, inc=1, device_id=where, device_id_type=MESH)

    p.column_first(greet, greet)
    expected = len(peers) + p.has_north.astype(jnp.int32) + p.has_south.astype(jnp.int32)
    mine = (p.here & p.inner).astype(jnp.int32)
    expected += p.ends.astype(jnp.int32) * (4 - mine)
    expected += (p.ends & p.inner).astype(jnp.int32) * (8 - p.here.astype(jnp.int32))

    sems = Sems(s["send"], s["recv"])

    def reduction(m):
        if m == "r11":
            names = ("local", "from_twin", "xs", "xr", "zs", "zr", "out")
            return LastReduction(p, sems, *(s[m + n] for n in names))
        names = ("local", "from_twin", "xs", "xr", "zs", "zr", "yr", "out")
        return Reduction(p, sems, True, *(s[m + n] for n in names))

    def lon_halo(m, d):
        names = ("", "packed", "plus", "minus", "got_plus", "got_minus")
        return LonHalo(p, sems, *(s[m + n] for n in names), d)

    def pull(m, w, d):
        names = ("minus", "", "plus")
        outs = ("wide_out", "packed_out", "wide_in", "packed_in")
        return Pull(p, sems, *(s[m + n] for n in names), s[w], *(s[m + n] for n in outs), s["total"], d)

    def activation(m, d):
        return Activation(p, sems, *(s[m + n] for n in ("", "packed", "got", "turned")), d)

    red = {m: reduction(m) for m in ("r22", "r12", "r21", "r11")}
    halos = {m: lon_halo(m, d) for m, d in (("g2", d2), ("q2", d2), ("g1", d1), ("q1", d1))}
    pulls = {
        m: pull(m, w, d) for m, w, d in (("g2", "w22", d2), ("q2", "w12", d2), ("g1", "w21", d1), ("q1", "w11", d1))
    }
    acts = {m: activation(m, d) for m, d in (("h2", d2), ("x2", d2), ("h1", d1), ("x1", d1))}

    def gate(b, d):
        @pl.loop(0, T // 4)
        def _(i):
            rows = pl.ds(i * 4, 4)
            pre = s["a" + b][rows].astype(F32)
            sigma = jax.nn.sigmoid(pre)
            s["h" + b][pl.ds(d + i * 4, 4)] = (pre * sigma).astype(BF)
            s["slope" + b][rows] = sigma * (1.0 + pre * (1.0 - sigma))

    def use_pre(b):
        def use(row, v):
            s["q" + b][pl.ds(row, 8)] = (v * s["slope" + b][pl.ds(row, 8)]).astype(BF)

        return use

    def use_x(b, into):
        def use(row, v):
            into[pl.ds(row, 8)] = (s["g" + b][pl.ds(row, 8)].astype(F32) + v).astype(BF)

        return use

    def weight(act, m, r, columns=(0, 1, 2)):
        names = (m + "minus", m, m + "plus")
        acts[act].weight_gradient([(c, s[names[c]]) for c in columns], s[r + "local"])

    for m in red:
        s[m + "local"][9 * 288 :] = jnp.zeros((ROWS - 9 * 288, 128), F32)
    loads["g2"].wait()
    pl.semaphore_wait(barrier, expected)
    halos["g2"].start()
    loads["a2"].wait()
    gate("2", d2)
    loads["a1"].wait()
    gate("1", d1)
    loads["x1"].wait()
    loads["x2"].wait()
    for name in ("w22", "w12", "w21", "w11"):
        loads[name].wait()

    turns = [s["turn"].at[k] for k in range(3)]

    halos["g2"].drain()
    acts["h2"].start()
    halos["g2"].arrive()
    pulls["g2"].send()
    pulls["g2"].stay()
    pulls["g2"].finish(use_pre("2"), turns[0])
    halos["q2"].start(turns[0])
    acts["h2"].arrive()
    weight("h2", "g2", "r22")
    red["r22"].go()
    halos["q2"].drain()
    acts["x2"].start()
    red["r22"].go()

    halos["q2"].arrive()
    pulls["q2"].send()
    pulls["q2"].stay()
    pulls["q2"].finish(use_x("2", s["g1"]), turns[1])
    halos["g1"].start(turns[1])
    acts["x2"].arrive()
    weight("x2", "q2", "r12")
    red["r12"].go()
    red["r22"].go()
    halos["g1"].drain()
    acts["x1"].start()
    acts["h1"].start()
    red["r12"].go()

    halos["g1"].arrive()
    pulls["g1"].send()
    pulls["g1"].stay()
    acts["h1"].arrive()
    weight("h1", "g1", "r21")
    red["r21"].go()
    red["r22"].go()
    pulls["g1"].finish(use_pre("1"), turns[2])
    halos["q1"].start(turns[2])
    red["r21"].go()
    red["r12"].go()
    red["r22"].go()
    acts["x1"].arrive()
    weight("x1", "q1", "r11", (1,))
    red["r22"].go()
    red["r12"].go()
    red["r21"].go()

    halos["q1"].arrive()
    weight("x1", "q1", "r11", (0, 2))
    red["r11"].go()
    pulls["q1"].send()
    red["r11"].go()
    pulls["q1"].stay()
    red["r22"].go()
    red["r12"].go()
    red["r21"].go()
    red["r11"].go()
    red["r12"].go()
    red["r21"].go()
    red["r22"].go()
    red["r11"].go()
    red["r21"].go()
    pulls["q1"].finish(use_x("1", s["dx"]))
    stores = [pltpu.make_async_copy(s["dx"], dx_out, s["store"].at[0])]
    stores[0].start()
    red["r12"].go()
    red["r21"].go()
    red["r11"].go()
    red["r12"].go()
    red["r11"].go()
    red["r21"].go()
    for k, (m, out) in enumerate((("r22", r22_out), ("r12", r12_out), ("r21", r21_out), ("r11", r11_out))):
        stores.append(pltpu.make_async_copy(s[m + "out"], out, s["store"].at[1 + k]))
        stores[-1].start()
    halos["q1"].drain()
    assert [part.step for part in red.values()] == [8, 8, 8, 6]
    for part in red.values():
        part.drain()
    for part in acts.values():
        part.halo.drain()
    for copy in stores:
        copy.wait()


def unpack(*refs):
    tile_in, *sums_in = refs[:5]
    tile_out, *sums_out = refs[5:10]
    tile, *buffers = refs[10:19]
    took, gave = refs[19:]
    reads = [pltpu.make_async_copy(a, b, took.at[k]) for k, (a, b) in enumerate(zip(sums_in, buffers[:4]))]
    reads.append(pltpu.make_async_copy(tile_in, tile, took.at[4]))
    writes = [pltpu.make_async_copy(a, b, gave.at[k]) for k, (a, b) in enumerate(zip(buffers[4:], sums_out))]
    writes.append(pltpu.make_async_copy(tile, tile_out, gave.at[4]))
    for copy in reads:
        copy.start()
    for k in range(4):
        reads[k].wait()

        @pl.loop(0, 9)
        def _(tap):
            base = pl.multiple_of(tap * 288, 32)
            wide = buffers[k][pl.ds(base, C)].astype(F32)
            rest = buffers[k][pl.ds(base + C, C // 2)].astype(F32)
            buffers[4 + k][tap, :, :128] = wide
            buffers[4 + k][tap, : C // 2, 128:] = rest[:, :64]
            buffers[4 + k][tap, C // 2 :, 128:] = rest[:, 64:]

        writes[k].start()
    reads[4].wait()
    writes[4].start()
    for copy in writes:
        copy.wait()


def local(x1, a1, x2, a2, g2, w11, w21, w12, w22):
    shapes = scratch()
    anywhere = pl.BlockSpec(memory_space=pl.ANY)
    packed = jax.ShapeDtypeStruct((ROWS, 128), BF)
    dx, *sums = pl.pallas_call(
        body,
        name="backward",
        out_shape=(jax.ShapeDtypeStruct((T, T, C), BF), packed, packed, packed, packed),
        in_specs=[anywhere] * 9,
        out_specs=[anywhere] * 5,
        scratch_shapes=list(shapes.values()),
        compiler_params=pltpu.CompilerParams(
            collective_id=0, has_side_effects=True, vmem_limit_bytes=60 * 1024 * 1024
        ),
    )(x1, a1, x2, a2, g2, w11, w21, w12, w22)
    full = jax.ShapeDtypeStruct((9, C, C), F32)
    return pl.pallas_call(
        unpack,
        name="unpack",
        out_shape=(jax.ShapeDtypeStruct((T, T, C), BF), full, full, full, full),
        in_specs=[anywhere] * 5,
        out_specs=[anywhere] * 5,
        scratch_shapes=[pltpu.VMEM((T, T, C), BF)]
        + [pltpu.VMEM((ROWS, 128), BF)] * 4
        + [pltpu.VMEM((9, C, C), F32)] * 4
        + [pltpu.SemaphoreType.DMA((5,)), pltpu.SemaphoreType.DMA((5,))],
    )(dx, *sums)


def solution(mesh):
    tile = P("lat", "lon", None)
    return jax.shard_map(
        local,
        mesh=mesh,
        in_specs=(tile,) * 5 + (P(),) * 4,
        out_specs=(tile, P(), P(), P(), P()),
        check_vma=False,
    )
```

```python
import jax
import jax.numpy as jnp
from jax import lax
from jax.experimental import pallas as pl
from jax.experimental.pallas import tpu as pltpu
from jax.sharding import PartitionSpec as P

C = 192
DILATION_FIRST = 16
DILATION_SECOND = 32
MESH = pl.DeviceIdType.MESH
BF = jnp.bfloat16
F32 = jnp.float32
T = 32
ROWS = 3072
HALF, QUART, PART, SHARD = ROWS // 2, ROWS // 8, ROWS // 32, ROWS // 64


class Place:
    def __init__(self):
        lon, lat = lax.axis_index("lon"), lax.axis_index("lat")
        self.lon, self.lat = lon, lat
        self.x, self.yh, self.z = lon // 16, (lon // 8) % 2, lon % 8
        self.yl, self.core = lat // 2, lat % 2
        self.y = self.yh * 2 + self.yl
        self.east = {"lon": (lon + 1) % 64, "lat": lat}
        self.west = {"lon": (lon + 63) % 64, "lat": lat}
        self.north = {"lon": lon, "lat": jnp.minimum(lat + 1, 3)}
        self.south = {"lon": lon, "lat": jnp.maximum(lat - 1, 0)}
        self.twin = {"lon": lon, "lat": lat + 1 - 2 * self.core}
        self.has_north, self.has_south = lat < 3, lat > 0
        self.ends = (self.z == 0) | (self.z == 7)
        self.inner = (lat == 1) | (lat == 2)
        top = (self.z == 7).astype(jnp.int32)
        half = 1 - top
        self.here = self.yh == half
        away = 2 * top - 1
        beside = (self.x + 4 + away) % 4
        self.column = jnp.where(self.here, self.x, beside)
        self.senders = (self.x * 16 + half * 8 + self.z, ((self.x + 4 - away) % 4) * 16 + top * 8 + self.z)

    def column_first(self, to_senders, to_column):
        @pl.when(self.ends & self.inner)
        def _():
            for k, lon in enumerate(self.senders):
                for lat in range(4):
                    other = jnp.logical_not(self.here & (self.lat == lat)) if k == 0 else self.ends
                    pl.when(other)(lambda lon=lon, lat=lat: to_senders({"lon": lon, "lat": lat}))

        if to_column is not None:

            @pl.when(self.ends)
            def _():
                for yh in range(2):
                    for lat in (1, 2):
                        other = jnp.logical_not(self.here & (self.yh == yh) & (self.lat == lat))
                        lon = self.column * 16 + yh * 8 + self.z
                        pl.when(other)(lambda lon=lon, lat=lat: to_column({"lon": lon, "lat": lat}))

    def at_x(self, k):
        x = (self.x + k) % 4
        return x, {"lon": x * 16 + self.lon % 16, "lat": self.lat}

    def at_y(self, k):
        y = (self.y + k) % 4
        return y, {"lon": self.x * 16 + (y // 2) * 8 + self.z, "lat": (y % 2) * 2 + self.core}

    def at_xy(self, k):
        x, y = (self.x + k // 4) % 4, (self.y + k % 4) % 4
        return x * 4 + y, {"lon": x * 16 + (y // 2) * 8 + self.z, "lat": (y % 2) * 2 + self.core}

    def at_z(self, k):
        z = (self.z + k) % 8
        return z, {"lon": self.lon - self.z + z, "lat": self.lat}


def remote(src, dst, send, recv, where):
    return pltpu.make_async_remote_copy(
        src_ref=src, dst_ref=dst, send_sem=send, recv_sem=recv, device_id=where, device_id_type=MESH
    )


class Sems:
    def __init__(self, send, recv):
        self.send, self.recv, self.n = send, recv, 0

    def take(self):
        k = self.n
        self.n += 1
        return self.send.at[k], self.recv.at[k]


class Reduction:
    def __init__(self, place, sems, along_x, local, from_twin, xs, xr, zs, zr, yr, out):
        self.p, self.local, self.from_twin = place, local, from_twin
        self.xs, self.xr, self.zs, self.zr, self.yr, self.out = xs, xr, zs, zr, yr, out
        p = place
        self.wide, at_wide = (p.x, p.at_x) if along_x else (p.y, p.at_y)
        thin, at_thin = (p.y, p.at_y) if along_x else (p.x, p.at_x)
        self.thin = thin
        self.mine = pl.multiple_of(p.core * HALF, HALF)
        other = pl.multiple_of((1 - p.core) * HALF, HALF)
        quarter = pl.multiple_of(self.mine + self.wide * QUART, QUART)
        self.shard = pl.ds(pl.multiple_of(quarter + p.z * SHARD, SHARD), SHARD)
        self.twin = [remote(local.at[pl.ds(other, HALF)], from_twin, *sems.take(), p.twin)]
        self.to_x = []
        for k in range(1, 4):
            x, where = at_wide(k)
            src = xs.at[pl.ds(pl.multiple_of(x * QUART, QUART), QUART)]
            self.to_x.append(remote(src, xr.at[k - 1], *sems.take(), where))
        self.to_z = []
        for k in range(1, 8):
            z, where = p.at_z(k)
            src = zs.at[pl.ds(pl.multiple_of(z * SHARD, SHARD), SHARD)]
            self.to_z.append(remote(src, zr.at[k - 1], *sems.take(), where))
        self.to_y = [remote(yr.at[thin], yr.at[thin], *sems.take(), at_thin(k)[1]) for k in range(1, 4)]
        ref = out.at[self.shard]
        self.all_z = [remote(ref, ref, *sems.take(), p.at_z(k)[1]) for k in range(1, 8)]
        ref = out.at[pl.ds(quarter, QUART)]
        self.all_x = [remote(ref, ref, *sems.take(), at_wide(k)[1]) for k in range(1, 4)]
        self.all_twin = []
        for k in range(4):
            ref = out.at[pl.ds(pl.multiple_of(self.mine + ((self.wide + 4 - k) % 4) * QUART, QUART), QUART)]
            self.all_twin.append(remote(ref, ref, *sems.take(), p.twin))
        self.step = 0

    def go(self):
        getattr(self, f"step{self.step}")()
        self.step += 1

    def start(self, copies):
        size = len(copies) + 1

        def hops(at):
            k = at + 1
            if size == 16:
                return min(k // 4, 4 - k // 4) + min(k % 4, 4 - k % 4)
            return min(k, size - k)

        for at in sorted(range(len(copies)), key=hops, reverse=True):
            copies[at].start()

    def arrive(self, copies):
        for copy in copies:
            copy.wait_recv()

    def step0(self):
        self.start(self.twin)

    def step1(self):
        self.arrive(self.twin)

        @pl.loop(0, HALF // 128)
        def _(i):
            rows = pl.ds(pl.multiple_of(i * 128, 128), 128)
            own = self.local[pl.ds(pl.multiple_of(self.mine + i * 128, 128), 128)]
            self.xs[rows] = (own + self.from_twin[rows]).astype(BF)

        self.start(self.to_x)

    def step2(self):
        self.arrive(self.to_x)
        total = self.xs[pl.ds(pl.multiple_of(self.wide * QUART, QUART), QUART)].astype(F32)
        for k in range(3):
            total = total + self.xr[k].astype(F32)
        self.zs[...] = total.astype(BF)
        self.start(self.to_z)

    def step3(self):
        self.arrive(self.to_z)
        total = self.zs[pl.ds(pl.multiple_of(self.p.z * SHARD, SHARD), SHARD)].astype(F32)
        for k in range(7):
            total = total + self.zr[k].astype(F32)
        self.yr[self.thin] = total
        self.start(self.to_y)

    def step4(self):
        self.arrive(self.to_y)
        self.out[self.shard] = ((self.yr[0] + self.yr[1]) + (self.yr[2] + self.yr[3])).astype(BF)
        self.start(self.all_z)

    def step5(self):
        self.arrive(self.all_z)
        self.start(self.all_x)
        self.all_twin[0].start()

    def step6(self):
        for k in range(3):
            self.all_x[k].wait_recv()
            self.all_twin[k + 1].start()

    def step7(self):
        self.arrive(self.all_twin)

    def drain(self):
        for copies in (self.twin, self.to_x, self.to_z, self.to_y, self.all_z, self.all_x, self.all_twin):
            for copy in copies:
                copy.wait_send()


class LastReduction(Reduction):
    def __init__(self, place, sems, local, from_twin, xs, xr, zs, zr, out):
        self.p, self.local, self.from_twin = place, local, from_twin
        self.xs, self.xr, self.zs, self.zr, self.out = xs, xr, zs, zr, out
        p = place
        self.mine = pl.multiple_of(p.core * HALF, HALF)
        other = pl.multiple_of((1 - p.core) * HALF, HALF)
        self.own = pl.multiple_of((p.x * 4 + p.y) * PART, PART)
        self.twin = [remote(local.at[pl.ds(other, HALF)], from_twin, *sems.take(), p.twin)]
        self.to_x = []
        for k in range(1, 16):
            xy, where = p.at_xy(k)
            src = xs.at[pl.ds(pl.multiple_of(xy * PART, PART), PART)]
            self.to_x.append(remote(src, xr.at[k - 1], *sems.take(), where))
        self.to_z = [remote(zs, zr.at[p.z], *sems.take(), p.at_z(k)[1]) for k in range(1, 8)]
        self.to_y = []
        self.shard = pl.ds(pl.multiple_of(self.mine + self.own, PART), PART)
        ref = out.at[self.shard]
        self.all_z = [remote(ref, ref, *sems.take(), p.at_xy(k)[1]) for k in range(1, 16)]
        self.all_x = []
        ref = out.at[pl.ds(self.mine, HALF)]
        self.all_twin = [remote(ref, ref, *sems.take(), p.twin)]
        self.step = 0

    def step2(self):
        self.arrive(self.to_x)
        total = self.xs[pl.ds(self.own, PART)].astype(F32)
        for k in range(15):
            total = total + self.xr[k].astype(F32)
        total = total.astype(BF)
        self.zs[...] = total
        self.zr[self.p.z] = total
        self.start(self.to_z)

    def step3(self):
        self.arrive(self.to_z)
        total = self.zr[0].astype(F32)
        for k in range(1, 8):
            total = total + self.zr[k].astype(F32)
        self.out[self.shard] = total.astype(BF)
        self.start(self.all_z)

    def step4(self):
        self.arrive(self.all_z)
        self.start(self.all_twin)

    def step5(self):
        self.arrive(self.all_twin)


def pack_rows(v, half):
    return jnp.concatenate([v[:half, :, 128:], v[half:, :, 128:]], axis=-1)


class LonHalo:
    def __init__(self, place, sems, tile, packed, plus, minus, got_plus, got_minus, d):
        self.p = place
        self.tile, self.packed, self.plus, self.minus, self.d = tile, packed, plus, minus, d
        self.got_plus, self.got_minus = got_plus, got_minus
        low, high = pl.ds(0, d), pl.ds(T - d, d)
        wide = pl.ds(0, 128)
        self.copies = [
            remote(tile.at[:, high, wide], plus.at[:, low, wide], *sems.take(), place.east),
            remote(tile.at[:, low, wide], minus.at[:, high, wide], *sems.take(), place.west),
            remote(packed.at[:, high], got_plus, *sems.take(), place.east),
            remote(packed.at[:, low], got_minus, *sems.take(), place.west),
        ]

    def start(self, turn=None):
        p = self.p
        late = [(p.z == z) if turn is not None else None for z in (7, 0, 7, 0)]

        def go(k):
            if late[k] is None:
                self.copies[k].start()
            else:
                pl.when(jnp.logical_not(late[k]))(self.copies[k].start)

        go(0)
        go(1)
        self.packed[...] = pack_rows(self.tile[...], T // 2)
        go(2)
        go(3)
        d = self.d
        if d < T:
            self.plus[:, d:, :] = self.tile[:, : T - d, :]
            self.minus[:, : T - d, :] = self.tile[:, d:, :]
        if turn is not None:

            @pl.when(p.ends)
            def _():
                pl.semaphore_wait(turn, 4 - (p.inner & p.here).astype(jnp.int32))

            for k in range(4):
                pl.when(late[k])(self.copies[k].start)

    def arrive(self):
        for copy in self.copies:
            copy.wait_recv()
        d, h = self.d, T // 2
        self.plus[:h, :d, 128:] = self.got_plus[:, :, :64]
        self.plus[h:, :d, 128:] = self.got_plus[:, :, 64:]
        self.minus[:h, T - d :, 128:] = self.got_minus[:, :, :64]
        self.minus[h:, T - d :, 128:] = self.got_minus[:, :, 64:]

    def drain(self):
        for copy in self.copies:
            copy.wait_send()


def pack_columns(v):
    return jnp.concatenate([v[:, : T // 2, 128:], v[:, T // 2 :, 128:]], axis=-1)


class LatPair:
    def __init__(self, place, copies_north, copies_south):
        self.p, self.to_north, self.to_south = place, copies_north, copies_south

    def start(self):
        lat = self.p.lat

        @pl.when(lat == 2)
        def _():
            for copy in self.to_south:
                copy.start()

        @pl.when(self.p.has_north)
        def _():
            for copy in self.to_north:
                copy.start()

        @pl.when(self.p.has_south & (lat != 2))
        def _():
            for copy in self.to_south:
                copy.start()

    def arrive(self):
        @pl.when(self.p.has_south)
        def _():
            for copy in self.to_north:
                copy.wait_recv()

        @pl.when(self.p.has_north)
        def _():
            for copy in self.to_south:
                copy.wait_recv()

    def drain(self):
        @pl.when(self.p.has_north)
        def _():
            for copy in self.to_north:
                copy.wait_send()

        @pl.when(self.p.has_south)
        def _():
            for copy in self.to_south:
                copy.wait_send()


class Activation:
    def __init__(self, place, sems, wide, packed, got, turned, d):
        self.p, self.wide, self.packed, self.got, self.turned, self.d = place, wide, packed, got, turned, d
        lanes = pl.ds(0, 128)
        top, bottom = pl.ds(d, d), pl.ds(T, d)
        self.halo = LatPair(
            place,
            [
                remote(wide.at[bottom, :, lanes], wide.at[pl.ds(0, d), :, lanes], *sems.take(), place.north),
                remote(packed.at[pl.ds(T - d, d)], got.at[0], *sems.take(), place.north),
            ],
            [
                remote(wide.at[top, :, lanes], wide.at[pl.ds(T + d, d), :, lanes], *sems.take(), place.south),
                remote(packed.at[pl.ds(0, d)], got.at[1], *sems.take(), place.south),
            ],
        )

    def start(self):
        d = self.d

        @pl.loop(0, 4)
        def _(i):
            v = self.wide[pl.ds(d + i * 8, 8)]
            self.packed[pl.ds(i * 8, 8)] = pack_columns(v)

        self.halo.start()

        @pl.when(jnp.logical_not(self.p.has_south))
        def _():
            self.wide[:d] = jnp.zeros((d, T, C), BF)

        @pl.when(jnp.logical_not(self.p.has_north))
        def _():
            self.wide[T + d :] = jnp.zeros((d, T, C), BF)

    def arrive(self):
        d, h = self.d, T // 2
        self.halo.arrive()

        @pl.when(self.p.has_south)
        def _():
            self.wide[:d, :h, 128:] = self.got[0, :, :, :64]
            self.wide[:d, h:, 128:] = self.got[0, :, :, 64:]

        @pl.when(self.p.has_north)
        def _():
            self.wide[T + d :, :h, 128:] = self.got[1, :, :, :64]
            self.wide[T + d :, h:, 128:] = self.got[1, :, :, 64:]

        @pl.loop(0, (T + 2 * d) // 8)
        def _(i):
            v = self.wide[pl.ds(i * 8, 8)].reshape(8 * T, C)
            self.turned[:, pl.ds(pl.multiple_of(i * 8 * T, 8 * T), 8 * T)] = v.T

    def weight_gradient(self, gradients, into):
        cells = T * T

        @pl.loop(0, 3)
        def _(r):
            start = pl.multiple_of(r * self.d * T, 512)
            turned = self.turned[:, pl.ds(start, cells)]
            for c, g in gradients:
                d = jnp.dot(turned, g[...].reshape(cells, C), preferred_element_type=F32)
                base = pl.multiple_of((3 * r + c) * 288, 32)
                into[pl.ds(base, C)] = d[:, :128]
                into[pl.ds(base + C, C // 2)] = jnp.concatenate([d[: C // 2, 128:], d[C // 2 :, 128:]], axis=1)


class Pull:
    def __init__(self, place, sems, minus, tile, plus, weights, wide_out, packed_out, wide_in, packed_in, total, d):
        self.p, self.g, self.w, self.d = place, (minus, tile, plus), weights, d
        self.wide_out, self.packed_out, self.wide_in, self.packed_in = wide_out, packed_out, wide_in, packed_in
        self.total = total
        self.halo = LatPair(
            place,
            [
                remote(wide_out.at[0], wide_in.at[0], *sems.take(), place.north),
                remote(packed_out.at[0], packed_in.at[0], *sems.take(), place.north),
            ],
            [
                remote(wide_out.at[1], wide_in.at[1], *sems.take(), place.south),
                remote(packed_out.at[1], packed_in.at[1], *sems.take(), place.south),
            ],
        )

    def partial(self, r, row, rows=8):
        total = None
        for c in range(3):
            g = self.g[c][pl.ds(row, rows)].reshape(rows * T, C)
            term = lax.dot_general(
                g, self.w[3 * (r + 1) + c], (((1,), (1,)), ((), ())), preferred_element_type=F32
            )
            total = term if total is None else total + term
        return total.reshape(rows, T, C)

    def send(self):
        d, p = self.d, self.p
        slots = ((p.has_north, 1, T - d, self.halo.to_north), (p.has_south, -1, 0, self.halo.to_south))
        for core, order in ((1, (0, 1)), (0, (1, 0))):
            for slot in order:
                there, r, first, copies = slots[slot]

                @pl.when((p.core == core) & there)
                def _(slot=slot, r=r, first=first, copies=copies):
                    @pl.loop(0, d // 16)
                    def _(i):
                        v = self.partial(r, first + i * 16, 16).astype(BF)
                        self.wide_out[slot, pl.ds(i * 16, 16)] = v[:, :, :128]
                        self.packed_out[slot, pl.ds(i * 16, 16)] = pack_columns(v)

                    for copy in copies:
                        copy.start()

        @pl.when(jnp.logical_not(self.p.has_south))
        def _():
            self.wide_in[0] = jnp.zeros(self.wide_in.shape[1:], BF)
            self.packed_in[0] = jnp.zeros(self.packed_in.shape[1:], BF)

        @pl.when(jnp.logical_not(self.p.has_north))
        def _():
            self.wide_in[1] = jnp.zeros(self.wide_in.shape[1:], BF)
            self.packed_in[1] = jnp.zeros(self.packed_in.shape[1:], BF)

    def stay(self):
        d = self.d

        @pl.loop(0, T // 8)
        def _(i):
            self.total[pl.ds(i * 8, 8)] = self.partial(0, i * 8)

        if d < T:

            @pl.loop(0, (T - d) // 8)
            def _(i):
                self.total[pl.ds(d + i * 8, 8)] += self.partial(1, i * 8)
                self.total[pl.ds(i * 8, 8)] += self.partial(-1, d + i * 8)

    def finish(self, use, turn=None):
        d = self.d
        self.halo.drain()
        if turn is not None:

            self.p.column_first(
                lambda where: pl.semaphore_signal(turn, inc=1, device_id=where, device_id_type=MESH), None
            )
        self.halo.arrive()

        def got(slot, row):
            w = self.wide_in[slot, pl.ds(row, 8)].astype(F32)
            q = self.packed_in[slot, pl.ds(row, 8)].astype(F32)
            return jnp.concatenate([w, jnp.concatenate([q[:, :, :64], q[:, :, 64:]], axis=1)], axis=-1)

        if d == T:

            @pl.loop(0, T // 8)
            def _(i):
                use(i * 8, self.total[pl.ds(i * 8, 8)] + got(0, i * 8) + got(1, i * 8))

        else:

            @pl.loop(0, d // 8)
            def _(i):
                use(i * 8, self.total[pl.ds(i * 8, 8)] + got(0, i * 8))
                use(T - d + i * 8, self.total[pl.ds(T - d + i * 8, 8)] + got(1, i * 8))


def scratch():
    v = pltpu.VMEM
    shapes = {}
    for b, d in (("1", DILATION_FIRST), ("2", DILATION_SECOND)):
        shapes["a" + b] = v((T, T, C), BF)
        shapes["slope" + b] = v((T, T, C), F32)
        for n in ("w1", "w2"):
            shapes[n + b] = v((9, C, C), BF)
        for n in ("h", "x"):
            shapes[n + b] = v((T + 2 * d, T, C), BF)
            shapes[n + b + "packed"] = v((T, T // 2, 128), BF)
            shapes[n + b + "got"] = v((2, d, T // 2, 128), BF)
            shapes[n + b + "turned"] = v((C, (T + 2 * d) * T), BF)
        for n in ("g", "q"):
            shapes[n + b] = v((T, T, C), BF)
            shapes[n + b + "packed"] = v((T // 2, T, 128), BF)
            for s in ("plus", "minus"):
                shapes[n + b + s] = v((T, T, C), BF)
                shapes[n + b + "got_" + s] = v((T // 2, d, 128), BF)
            for s in ("wide_out", "wide_in"):
                shapes[n + b + s] = v((2, d, T, 128), BF)
            for s in ("packed_out", "packed_in"):
                shapes[n + b + s] = v((2, d, T // 2, 128), BF)
        for n in ("1", "2"):
            m = "r" + n + b
            shapes[m + "local"] = v((ROWS, 128), F32)
            shapes[m + "from_twin"] = v((HALF, 128), F32)
            last = m == "r11"
            shapes[m + "xs"] = v((HALF, 128), BF)
            shapes[m + "xr"] = v((15, PART, 128) if last else (3, QUART, 128), BF)
            shapes[m + "zs"] = v((PART if last else QUART, 128), BF)
            shapes[m + "zr"] = v((8, PART, 128) if last else (7, SHARD, 128), BF)
            if not last:
                shapes[m + "yr"] = v((4, SHARD, 128), F32)
            shapes[m + "out"] = v((ROWS, 128), BF)
    shapes["total"] = v((T, T, C), F32)
    shapes["dx"] = v((T, T, C), BF)
    shapes["load"] = pltpu.SemaphoreType.DMA((9,))
    shapes["store"] = pltpu.SemaphoreType.DMA((5,))
    shapes["send"] = pltpu.SemaphoreType.DMA((192,))
    shapes["turn"] = pltpu.SemaphoreType.REGULAR((3,))
    shapes["recv"] = pltpu.SemaphoreType.DMA((192,))
    return shapes


NAMES = tuple(scratch())


def body(x1, a1, x2, a2, g2, w11, w21, w12, w22, dx_out, r11_out, r21_out, r12_out, r22_out, *refs):
    s = dict(zip(NAMES, refs))
    p = Place()
    loads = {}
    d1, d2 = DILATION_FIRST, DILATION_SECOND
    for k, (name, src, dst) in enumerate(
        (
            ("g2", g2, s["g2"]),
            ("a2", a2, s["a2"]),
            ("x2", x2, s["x2"].at[pl.ds(d2, T)]),
            ("w22", w22, s["w22"]),
            ("a1", a1, s["a1"]),
            ("x1", x1, s["x1"].at[pl.ds(d1, T)]),
            ("w12", w12, s["w12"]),
            ("w21", w21, s["w21"]),
            ("w11", w11, s["w11"]),
        )
    ):
        loads[name] = pltpu.make_async_copy(src, dst, s["load"].at[k])
        loads[name].start()

    barrier = pltpu.get_barrier_semaphore()
    peers = [p.east, p.west, p.twin]
    peers += [p.at_xy(k)[1] for k in range(1, 16)]
    peers += [p.at_z(k)[1] for k in range(1, 8)]
    for where in peers:
        pl.semaphore_signal(barrier, inc=1, device_id=where, device_id_type=MESH)
    for cond, where in ((p.has_north, p.north), (p.has_south, p.south)):

        @pl.when(cond)
        def _():
            pl.semaphore_signal(barrier, inc=1, device_id=where, device_id_type=MESH)

    def greet(where):
        pl.semaphore_signal(barrier, inc=1, device_id=where, device_id_type=MESH)

    p.column_first(greet, greet)
    expected = len(peers) + p.has_north.astype(jnp.int32) + p.has_south.astype(jnp.int32)
    mine = (p.here & p.inner).astype(jnp.int32)
    expected += p.ends.astype(jnp.int32) * (4 - mine)
    expected += (p.ends & p.inner).astype(jnp.int32) * (8 - p.here.astype(jnp.int32))

    sems = Sems(s["send"], s["recv"])

    def reduction(m):
        if m == "r11":
            names = ("local", "from_twin", "xs", "xr", "zs", "zr", "out")
            return LastReduction(p, sems, *(s[m + n] for n in names))
        names = ("local", "from_twin", "xs", "xr", "zs", "zr", "yr", "out")
        return Reduction(p, sems, True, *(s[m + n] for n in names))

    def lon_halo(m, d):
        names = ("", "packed", "plus", "minus", "got_plus", "got_minus")
        return LonHalo(p, sems, *(s[m + n] for n in names), d)

    def pull(m, w, d):
        names = ("minus", "", "plus")
        outs = ("wide_out", "packed_out", "wide_in", "packed_in")
        return Pull(p, sems, *(s[m + n] for n in names), s[w], *(s[m + n] for n in outs), s["total"], d)

    def activation(m, d):
        return Activation(p, sems, *(s[m + n] for n in ("", "packed", "got", "turned")), d)

    red = {m: reduction(m) for m in ("r22", "r12", "r21", "r11")}
    halos = {m: lon_halo(m, d) for m, d in (("g2", d2), ("q2", d2), ("g1", d1), ("q1", d1))}
    pulls = {
        m: pull(m, w, d) for m, w, d in (("g2", "w22", d2), ("q2", "w12", d2), ("g1", "w21", d1), ("q1", "w11", d1))
    }
    acts = {m: activation(m, d) for m, d in (("h2", d2), ("x2", d2), ("h1", d1), ("x1", d1))}

    def gate(b, d):
        @pl.loop(0, T // 4)
        def _(i):
            rows = pl.ds(i * 4, 4)
            pre = s["a" + b][rows].astype(F32)
            sigma = jax.nn.sigmoid(pre)
            s["h" + b][pl.ds(d + i * 4, 4)] = (pre * sigma).astype(BF)
            s["slope" + b][rows] = sigma * (1.0 + pre * (1.0 - sigma))

    def use_pre(b):
        def use(row, v):
            s["q" + b][pl.ds(row, 8)] = (v * s["slope" + b][pl.ds(row, 8)]).astype(BF)

        return use

    def use_x(b, into):
        def use(row, v):
            into[pl.ds(row, 8)] = (s["g" + b][pl.ds(row, 8)].astype(F32) + v).astype(BF)

        return use

    def weight(act, m, r, columns=(0, 1, 2)):
        names = (m + "minus", m, m + "plus")
        acts[act].weight_gradient([(c, s[names[c]]) for c in columns], s[r + "local"])

    for m in red:
        s[m + "local"][9 * 288 :] = jnp.zeros((ROWS - 9 * 288, 128), F32)
    loads["g2"].wait()
    pl.semaphore_wait(barrier, expected)
    halos["g2"].start()
    loads["a2"].wait()
    gate("2", d2)
    loads["a1"].wait()
    gate("1", d1)
    loads["x1"].wait()
    loads["x2"].wait()
    for name in ("w22", "w12", "w21", "w11"):
        loads[name].wait()

    turns = [s["turn"].at[k] for k in range(3)]

    halos["g2"].drain()
    acts["h2"].start()
    halos["g2"].arrive()
    pulls["g2"].send()
    pulls["g2"].stay()
    pulls["g2"].finish(use_pre("2"), turns[0])
    halos["q2"].start(turns[0])
    acts["h2"].arrive()
    weight("h2", "g2", "r22")
    red["r22"].go()
    halos["q2"].drain()
    acts["x2"].start()
    red["r22"].go()

    halos["q2"].arrive()
    pulls["q2"].send()
    pulls["q2"].stay()
    pulls["q2"].finish(use_x("2", s["g1"]), turns[1])
    halos["g1"].start(turns[1])
    acts["x2"].arrive()
    weight("x2", "q2", "r12")
    red["r12"].go()
    red["r22"].go()
    halos["g1"].drain()
    acts["x1"].start()
    acts["h1"].start()
    red["r12"].go()

    halos["g1"].arrive()
    pulls["g1"].send()
    pulls["g1"].stay()
    acts["h1"].arrive()
    weight("h1", "g1", "r21")
    red["r21"].go()
    red["r22"].go()
    pulls["g1"].finish(use_pre("1"), turns[2])
    halos["q1"].start(turns[2])
    red["r21"].go()
    red["r12"].go()
    red["r22"].go()
    acts["x1"].arrive()
    weight("x1", "q1", "r11", (1,))
    red["r22"].go()
    red["r12"].go()
    red["r21"].go()

    halos["q1"].arrive()
    weight("x1", "q1", "r11", (0, 2))
    red["r11"].go()
    pulls["q1"].send()
    red["r11"].go()
    red["r22"].go()
    red["r12"].go()
    red["r21"].go()
    pulls["q1"].stay()
    red["r21"].go()
    red["r12"].go()
    red["r11"].go()
    red["r22"].go()
    red["r21"].go()
    red["r11"].go()
    pulls["q1"].finish(use_x("1", s["dx"]))
    stores = [pltpu.make_async_copy(s["dx"], dx_out, s["store"].at[0])]
    stores[0].start()
    red["r12"].go()
    red["r21"].go()
    red["r11"].go()
    red["r12"].go()
    red["r11"].go()
    red["r21"].go()
    for k, (m, out) in enumerate((("r22", r22_out), ("r12", r12_out), ("r21", r21_out), ("r11", r11_out))):
        stores.append(pltpu.make_async_copy(s[m + "out"], out, s["store"].at[1 + k]))
        stores[-1].start()
    halos["q1"].drain()
    assert [part.step for part in red.values()] == [8, 8, 8, 6]
    for part in red.values():
        part.drain()
    for part in acts.values():
        part.halo.drain()
    for copy in stores:
        copy.wait()


def unpack(*refs):
    tile_in, *sums_in = refs[:5]
    tile_out, *sums_out = refs[5:10]
    tile, *buffers = refs[10:19]
    took, gave = refs[19:]
    reads = [pltpu.make_async_copy(a, b, took.at[k]) for k, (a, b) in enumerate(zip(sums_in, buffers[:4]))]
    reads.append(pltpu.make_async_copy(tile_in, tile, took.at[4]))
    writes = [pltpu.make_async_copy(a, b, gave.at[k]) for k, (a, b) in enumerate(zip(buffers[4:], sums_out))]
    writes.append(pltpu.make_async_copy(tile, tile_out, gave.at[4]))
    for copy in reads:
        copy.start()
    for k in range(4):
        reads[k].wait()

        @pl.loop(0, 9)
        def _(tap):
            base = pl.multiple_of(tap * 288, 32)
            wide = buffers[k][pl.ds(base, C)].astype(F32)
            rest = buffers[k][pl.ds(base + C, C // 2)].astype(F32)
            buffers[4 + k][tap, :, :128] = wide
            buffers[4 + k][tap, : C // 2, 128:] = rest[:, :64]
            buffers[4 + k][tap, C // 2 :, 128:] = rest[:, 64:]

        writes[k].start()
    reads[4].wait()
    writes[4].start()
    for copy in writes:
        copy.wait()


def local(x1, a1, x2, a2, g2, w11, w21, w12, w22):
    shapes = scratch()
    anywhere = pl.BlockSpec(memory_space=pl.ANY)
    packed = jax.ShapeDtypeStruct((ROWS, 128), BF)
    dx, *sums = pl.pallas_call(
        body,
        name="backward",
        out_shape=(jax.ShapeDtypeStruct((T, T, C), BF), packed, packed, packed, packed),
        in_specs=[anywhere] * 9,
        out_specs=[anywhere] * 5,
        scratch_shapes=list(shapes.values()),
        compiler_params=pltpu.CompilerParams(
            collective_id=0, has_side_effects=True, vmem_limit_bytes=60 * 1024 * 1024
        ),
    )(x1, a1, x2, a2, g2, w11, w21, w12, w22)
    full = jax.ShapeDtypeStruct((9, C, C), F32)
    return pl.pallas_call(
        unpack,
        name="unpack",
        out_shape=(jax.ShapeDtypeStruct((T, T, C), BF), full, full, full, full),
        in_specs=[anywhere] * 5,
        out_specs=[anywhere] * 5,
        scratch_shapes=[pltpu.VMEM((T, T, C), BF)]
        + [pltpu.VMEM((ROWS, 128), BF)] * 4
        + [pltpu.VMEM((9, C, C), F32)] * 4
        + [pltpu.SemaphoreType.DMA((5,)), pltpu.SemaphoreType.DMA((5,))],
    )(dx, *sums)


def solution(mesh):
    tile = P("lat", "lon", None)
    return jax.shard_map(
        local,
        mesh=mesh,
        in_specs=(tile,) * 5 + (P(),) * 4,
        out_specs=(tile, P(), P(), P(), P()),
        check_vma=False,
    )
```
